128 devices in a mesh: row: 16 (over y, z), col: 8 (over x, core).
Axes of the slice: x: 4, y: 4, z: 4, core: 2. Of those that a mesh axis runs over, the one named last changes fastest.
Arguments:
- panel: float32 [1572864, 256], P(('row', 'col')), may hold values from -2000 to 2000, as said below
Outputs:
- basis: float32 [1572864, 256], P(('row', 'col'))
- factor: float32 [256, 256], replicated
The draws below stay inside these ranges and needn't reach their ends.
Inputs may be any that keep to these rules, and one draw needn't show every extreme that they name: `panel`: Real-valued entries of full column rank.
All inputs are finite; a program needn't handle non-finite values.
Results may differ from the reference program's by a relative error of at most 0.0003.
Values sent between devices are 32-bit elements; how exact they have to be, the bound alone decides.
No kernel may reach another device: no remote copies, remote signals or barrier semaphores. Data moves between devices by JAX's collectives and lax.ppermute only.
A program may use at most 128 MiB of HBM per device.

```python
import jax
import jax.numpy as jnp
from jax import lax

K = 256
ROWS = 1572864


def draw_panel(key, part):
    keys = jax.random.split(key, 7)
    place = jnp.arange(ROWS, dtype=jnp.float32) / ROWS
    col_scale = jnp.exp(jax.random.uniform(keys[1], (K,), jnp.float32) * jnp.log(10.0))
    order = jax.random.permutation(keys[5], K)
    half_cols = K // 2
    leading = order[:half_cols]
    following = order[half_cols:]
    partner = jnp.arange(K, dtype=jnp.int32).at[following].set(leading.astype(jnp.int32))
    paired = jnp.zeros((K,), jnp.float32).at[following].set(1.0)
    low_end = 0.004
    high_end = 0.012
    spread = jax.random.uniform(keys[6], (K,), jnp.float32)
    offset = jnp.exp(jnp.log(low_end) + spread * (jnp.log(high_end) - jnp.log(low_end)))
    own_weight = jnp.where(paired > 0.5, offset, 1.0)
    base = jnp.clip(jax.random.normal(keys[0], (ROWS, K), jnp.float32), -6.0, 6.0)
    row_scale = jnp.exp(jax.random.uniform(keys[2], (ROWS,), jnp.float32) * jnp.log(10.0)) * (1.0 + 2.0 * place)
    mixed = base * own_weight[None, :] + jnp.take(base, partner, axis=1) * paired[None, :]
    values = mixed * col_scale[None, :] * row_scale[:, None]
    return values


def setup_inputs(seed: int = 0) -> dict:
    arg_keys = jax.random.split(jax.random.key(seed), 2)
    return {
        "panel": draw_panel(jax.random.fold_in(arg_keys[1], 71), 0),
    }


def one_pass(matrix):
    gram = jnp.dot(matrix.T.astype(jnp.float32), matrix.astype(jnp.float32), precision=lax.Precision.HIGHEST, preferred_element_type=jnp.float32)
    lower = jnp.linalg.cholesky(gram)
    identity = jnp.eye(matrix.shape[1], dtype=gram.dtype)
    inverse = lax.linalg.triangular_solve(lower, identity, left_side=True, lower=True)
    result = jnp.dot(matrix.astype(jnp.float32), inverse.T.astype(jnp.float32), precision=lax.Precision.HIGHEST, preferred_element_type=jnp.float32)
    return (result, lower)

def reference(panel):
    first, lower_one = one_pass(panel)
    second, lower_two = one_pass(first)
    scale = jnp.sqrt(jnp.float32(ROWS))
    combined = jnp.dot(lower_one.astype(jnp.float32), lower_two.astype(jnp.float32), precision=lax.Precision.HIGHEST, preferred_element_type=jnp.float32)
    return (second * scale, combined.T / scale)
```

```python
import functools
import jax
import jax.numpy as jnp
from jax import lax
from jax.experimental import pallas as pl
from jax.experimental.pallas import tpu as pltpu
from jax.sharding import PartitionSpec as P

K = 256
H = 128
HALF = 136
F32 = jnp.float32
BF16 = jnp.bfloat16
VMEM_WHOLE = pl.BlockSpec(memory_space=pltpu.VMEM)


def split2(x):
    hi = x.astype(BF16)
    return hi, (x - hi.astype(F32)).astype(BF16)


def split3(x):
    hi = x.astype(BF16)
    rest = x - hi.astype(F32)
    mid = rest.astype(BF16)
    return hi, mid, (rest - mid.astype(F32)).astype(BF16)


def dot_tn(a, b):
    return lax.dot_general(a, b, (((0,), (0,)), ((), ())), preferred_element_type=F32)


def dot_nn(a, b):
    return lax.dot_general(a, b, (((1,), (0,)), ((), ())), preferred_element_type=F32)


def dot_nt(a, b):
    return lax.dot_general(a, b, (((1,), (1,)), ((), ())), preferred_element_type=F32)


def iotas(shape):
    return lax.broadcasted_iota(jnp.int32, shape, 0), lax.broadcasted_iota(jnp.int32, shape, 1)


def core_index():
    return lax.rem(lax.axis_index("col"), 2)


def pack(gram, keep_ref, send_ref):
    i, j = iotas((H, H))
    low = gram[H:, H:]
    top = jnp.where(i >= j, gram[:H, :H], low)
    diag = jnp.sum(jnp.where(i == j, low, 0.0), axis=0, keepdims=True)
    tail = jnp.broadcast_to(diag, (8, H))
    core = core_index()

    def put(first_ref, second_ref):
        first_ref[0:H, :] = top
        first_ref[H:HALF, :] = tail
        second_ref[0:H, :] = gram[H:, :H]
        second_ref[H:HALF, :] = jnp.zeros((8, H), F32)

    @pl.when(core == 0)
    def _():
        put(keep_ref, send_ref)

    @pl.when(core == 1)
    def _():
        put(send_ref, keep_ref)


def unpack(mine_ref, other_ref, out_ref):
    core = core_index()
    i, j = iotas((H, H))

    def get(first_ref, second_ref):
        top = first_ref[0:H, :]
        topt = top.T
        diag = first_ref[H:H + 1, :]
        side = second_ref[0:H, :]
        out_ref[0:H, 0:H] = jnp.where(i >= j, top, topt)
        corner = jnp.where(i < j, top, topt)
        out_ref[H:, H:] = jnp.where(i == j, jnp.broadcast_to(diag, (H, H)), corner)
        out_ref[H:, 0:H] = side
        out_ref[0:H, H:] = side.T

    @pl.when(core == 0)
    def _():
        get(mine_ref, other_ref)

    @pl.when(core == 1)
    def _():
        get(other_ref, mine_ref)


def gram_kernel(steps, x_ref, keep_ref, send_ref, acc):
    step = pl.program_id(0)

    @pl.when(step == 0)
    def _():
        acc[...] = jnp.zeros_like(acc)

    h, m = split2(x_ref[...])
    acc[:, :2 * K] += dot_tn(h, jnp.concatenate([h, m], axis=1))
    acc[:, 2 * K:] += dot_tn(m, m)

    @pl.when(step == steps - 1)
    def _():
        cross = acc[:, K:2 * K]
        pack(acc[:, :K] + (cross + cross.T) + acc[:, 2 * K:], keep_ref, send_ref)


def gram_call(x, rows):
    steps = x.shape[0] // rows
    half = jax.ShapeDtypeStruct((HALF, H), F32)
    return pl.pallas_call(
        functools.partial(gram_kernel, steps),
        out_shape=(half, half),
        grid=(steps,),
        in_specs=[pl.BlockSpec((rows, K), lambda i: (i, 0))],
        out_specs=[pl.BlockSpec((HALF, H), lambda i: (0, 0))] * 2,
        scratch_shapes=[pltpu.VMEM((K, 3 * K), F32)],
        name="gram_one",
    )(x)


def first_kernel(steps, x_ref, w_ref, first_ref, keep_ref, send_ref, acc):
    step = pl.program_id(0)

    @pl.when(step == 0)
    def _():
        acc[...] = jnp.zeros_like(acc)

    h, m, l = split3(x_ref[...])
    first = dot_nn(jnp.concatenate([h, m, l, h, m], axis=1), w_ref[...])
    first_ref[...] = first
    fh, fm = split2(first)
    acc[...] += dot_tn(fh, jnp.concatenate([fh, fm], axis=1))

    @pl.when(step == steps - 1)
    def _():
        cross = acc[:, K:]
        pack(acc[:, :K] + (cross + cross.T), keep_ref, send_ref)


def first_call(x, w, rows):
    steps = x.shape[0] // rows
    half = jax.ShapeDtypeStruct((HALF, H), F32)
    return pl.pallas_call(
        functools.partial(first_kernel, steps),
        out_shape=(jax.ShapeDtypeStruct(x.shape, F32), half, half),
        grid=(steps,),
        in_specs=[pl.BlockSpec((rows, K), lambda i: (i, 0)), VMEM_WHOLE],
        out_specs=[pl.BlockSpec((rows, K), lambda i: (i, 0))] + [pl.BlockSpec((HALF, H), lambda i: (0, 0))] * 2,
        scratch_shapes=[pltpu.VMEM((K, 2 * K), F32)],
        name="first_and_gram_two",
    )(x, w)


def basis_kernel(scale, f_ref, c_ref, out_ref):
    first = f_ref[...]
    h, m = split2(first)
    out_ref[...] = (first + dot_nn(jnp.concatenate([h, m, h], axis=1), c_ref[...])) * scale


def basis_call(first, c, rows, scale):
    return pl.pallas_call(
        functools.partial(basis_kernel, scale),
        out_shape=jax.ShapeDtypeStruct(first.shape, F32),
        grid=(first.shape[0] // rows,),
        in_specs=[pl.BlockSpec((rows, K), lambda i: (i, 0)), VMEM_WHOLE],
        out_specs=pl.BlockSpec((rows, K), lambda i: (i, 0)),
        name="basis",
    )(first, c)


B = 32
S = 8


def eliminate(rows_a):
    rows_a = list(rows_a)
    width = rows_a[0].shape[1]
    sub = lax.broadcasted_iota(jnp.int32, (S, H), 0)
    for s in range(B // S):
        cols = [jnp.broadcast_to(rows_a[s][:, S * s + k:S * s + k + 1], (S, H)) for k in range(S)]
        x = rows_a[s]
        pivots, factors, us = [], [], []
        for j in range(S):
            r = jnp.broadcast_to(lax.rsqrt(cols[j][j:j + 1, :]), (S, H))
            lj = jnp.where(sub >= j, cols[j] * r, 0.0)
            fac = [None] * S
            for k in range(j + 1, S):
                fac[k] = jnp.broadcast_to(lj[k:k + 1, :], (S, H))
                cols[k] = cols[k] - lj * fac[k]
            u = jnp.broadcast_to(x[j:j + 1, :], (S, width)) * jnp.concatenate([r] * (width // H), axis=1)
            below = jnp.concatenate([jnp.where(sub > j, lj, 0.0)] * (width // H), axis=1)
            here = jnp.concatenate([sub == j] * (width // H), axis=1)
            x = jnp.where(here, u, x - below * u)
            pivots.append(r)
            factors.append(fac)
            us.append(u)
        rows_a[s] = x
        for q in range(s + 1, B // S):
            y = rows_a[q]
            c = [jnp.broadcast_to(y[:, S * s + k:S * s + k + 1], (S, H)) for k in range(S)]
            for j in range(S):
                lj = c[j] * pivots[j]
                for k in range(j + 1, S):
                    c[k] = c[k] - lj * factors[j][k]
                y = y - jnp.concatenate([lj] * (width // H), axis=1) * us[j]
            rows_a[q] = y
    return rows_a


def factorize(t_ref):
    def block(b, carry):
        r0 = pl.multiple_of(b * B, B)
        lane0 = pl.multiple_of(lax.div(b, H // B) * H, H)
        shift = lax.rem(b, H // B) * B
        d = t_ref[pl.ds(r0, B), pl.ds(lane0, H)]
        d = pltpu.roll(d, lax.rem(H - shift, H), 1)
        r = t_ref[pl.ds(r0, B), :]
        full = jnp.concatenate([d, r], axis=1)
        out = eliminate([full[S * s:S * s + S] for s in range(B // S)])
        u = jnp.concatenate([o[:, H:] for o in out], axis=0)
        t_ref[pl.ds(r0, B), :] = u
        lane = lax.broadcasted_iota(jnp.int32, (B, K), 1)
        left = jnp.where(lane >= r0 + B, u[:, :K], 0.0)
        lh, lm, ll = split3(left)
        uh, um, ul = split3(u)
        upd = dot_tn(
            jnp.concatenate([lh, lh, lm, lm, lh, ll], axis=0),
            jnp.concatenate([uh, um, uh, um, ul, uh], axis=0),
        )
        t_ref[...] -= upd
        return carry

    lax.fori_loop(0, K // B, block, 0)


def load_augmented(mine_ref, other_ref, t_ref):
    unpack(mine_ref, other_ref, t_ref.at[:, 0:K])
    i, j = iotas((K, K))
    t_ref[:, K:] = jnp.where(i == j, 1.0, 0.0)


def chol_one_kernel(mine_ref, other_ref, w_ref, upper_ref, t_ref):
    load_augmented(mine_ref, other_ref, t_ref)
    factorize(t_ref)
    i, j = iotas((K, K))
    upper_ref[...] = jnp.where(i <= j, t_ref[:, :K], 0.0)
    wt = jnp.where(i >= j, t_ref[:, K:], 0.0).T
    h, m = split2(wt)
    w_ref[0:K, :] = h
    w_ref[K:2 * K, :] = h
    w_ref[2 * K:3 * K, :] = h
    w_ref[3 * K:4 * K, :] = m
    w_ref[4 * K:5 * K, :] = m


def chol_one_call(mine, other):
    return pl.pallas_call(
        chol_one_kernel,
        out_shape=(jax.ShapeDtypeStruct((5 * K, K), BF16), jax.ShapeDtypeStruct((K, K), F32)),
        in_specs=[VMEM_WHOLE] * 2,
        out_specs=[VMEM_WHOLE] * 2,
        scratch_shapes=[pltpu.VMEM((K, 2 * K), F32)],
        name="factor_one",
    )(mine, other)


TOL = 1e-7


def largest(x):
    return jnp.max(jnp.abs(x))


def chol_two_kernel(scale, mine_ref, other_ref, upper_ref, c_ref, factor_ref, g_ref, x_ref, z_ref, t_ref):
    unpack(mine_ref, other_ref, g_ref)
    i, j = iotas((K, K))
    eye = jnp.where(i == j, 1.0, 0.0)
    half_low = jnp.where(i > j, 1.0, jnp.where(i == j, 0.5, 0.0))

    x_ref[...] = (g_ref[...] - eye) * half_low

    def x_more(state):
        step, change = state
        return jnp.logical_and(step < 10, jnp.logical_not(change <= TOL))

    def x_next(state):
        old = x_ref[...]
        h, m = split2(old)
        square = dot_nt(jnp.concatenate([h, h, m], axis=1), jnp.concatenate([h, m, h], axis=1))
        new = (g_ref[...] - eye - square) * half_low
        x_ref[...] = new
        return state[0] + 1, largest(new - old)

    _, change = lax.while_loop(x_more, x_next, (jnp.int32(0), jnp.float32(1.0)))
    x = x_ref[...]
    z_ref[...] = -x

    def residual():
        z = z_ref[...]
        xh, xm = split2(x_ref[...])
        zh, zm = split2(z)
        prod = dot_nn(jnp.concatenate([xh, xh, xm], axis=1), jnp.concatenate([zh, zm, zh], axis=0))
        return -(x_ref[...] + z + prod)

    def z_more(state):
        step, size = state
        return jnp.logical_and(step < 6, jnp.logical_not(size <= TOL))

    def z_next(state):
        r = residual()
        z = z_ref[...]
        rh, rm = split2(r)
        zh, zm = split2(z)
        z_ref[...] = z + r + dot_nn(jnp.concatenate([zh, zh, zm], axis=1), jnp.concatenate([rh, rm, rh], axis=0))
        return state[0] + 1, largest(r) * largest(r) * 256.0

    _, size = lax.while_loop(z_more, z_next, (jnp.int32(0), jnp.float32(1.0)))
    lowest = jnp.min(jnp.where(i == j, x, 0.0))
    good = jnp.logical_and(jnp.logical_and(change <= TOL, size <= TOL), lowest > -0.5)

    @pl.when(jnp.logical_not(good))
    def _():
        t_ref[:, :K] = g_ref[...]
        t_ref[:, K:] = eye
        factorize(t_ref)
        x_ref[...] = jnp.where(i <= j, t_ref[:, :K], 0.0).T - eye
        z_ref[...] = jnp.where(i >= j, t_ref[:, K:], 0.0) - eye

    ch, cm = split2(z_ref[...].T)
    c_ref[0:K, :] = ch
    c_ref[K:2 * K, :] = ch
    c_ref[2 * K:3 * K, :] = cm
    u1 = upper_ref[...]
    uh, um = split2(u1)
    xh, xm = split2(x_ref[...])
    prod = dot_tn(jnp.concatenate([xh, xh, xm], axis=0), jnp.concatenate([uh, um, uh], axis=0))
    factor_ref[...] = (u1 + prod) / scale


def chol_two_call(mine, other, upper, scale):
    return pl.pallas_call(
        functools.partial(chol_two_kernel, scale),
        out_shape=(jax.ShapeDtypeStruct((3 * K, K), BF16), jax.ShapeDtypeStruct((K, K), F32)),
        in_specs=[VMEM_WHOLE] * 3,
        out_specs=[VMEM_WHOLE] * 2,
        scratch_shapes=[pltpu.VMEM((K, K), F32)] * 3 + [pltpu.VMEM((K, 2 * K), F32)],
        name="factor_two",
    )(mine, other, upper)


def swap(value, axis, distance):
    return lax.ppermute(value, axis, [(i, i ^ distance) for i in range(lax.axis_size(axis))])


def sum_over(value, axis, step):
    a, b, c = [swap(value, axis, step * d) for d in (1, 2, 3)]
    return (value + a) + (b + c)


def reduce_gram(keep, send):
    value = keep + swap(send, "col", 1)
    value = sum_over(value, "col", 2)
    value = sum_over(value, "row", 1)
    value = sum_over(value, "row", 4)
    return value, swap(value, "col", 1)


ROWS_PER_STEP = 2048


def shards(panel):
    total_rows = panel.shape[0] * lax.axis_size("row") * lax.axis_size("col")
    scale = float(total_rows) ** 0.5
    mine, other = reduce_gram(*gram_call(panel, ROWS_PER_STEP))
    w, upper = chol_one_call(mine, other)
    first, keep, send = first_call(panel, w, ROWS_PER_STEP)
    mine, other = reduce_gram(keep, send)
    c, factor = chol_two_call(mine, other, upper, scale)
    return basis_call(first, c, ROWS_PER_STEP, scale), factor


def solution(mesh):
    return jax.shard_map(
        shards,
        mesh=mesh,
        in_specs=(P(("row", "col"), None),),
        out_specs=(P(("row", "col"), None), P()),
        check_vma=False,
    )
```

```python
import functools
import jax
import jax.numpy as jnp
from jax import lax
from jax.experimental import pallas as pl
from jax.experimental.pallas import tpu as pltpu
from jax.sharding import PartitionSpec as P

K = 256
H = 128
HALF = 136
F32 = jnp.float32
BF16 = jnp.bfloat16
VMEM_WHOLE = pl.BlockSpec(memory_space=pltpu.VMEM)


def params(mib):
    return pltpu.CompilerParams(vmem_limit_bytes=mib << 20)


def split2(x):
    hi = x.astype(BF16)
    return hi, (x - hi.astype(F32)).astype(BF16)


def split3(x):
    hi = x.astype(BF16)
    rest = x - hi.astype(F32)
    mid = rest.astype(BF16)
    return hi, mid, (rest - mid.astype(F32)).astype(BF16)


def dot_tn(a, b):
    return lax.dot_general(a, b, (((0,), (0,)), ((), ())), preferred_element_type=F32)


def dot_nn(a, b):
    return lax.dot_general(a, b, (((1,), (0,)), ((), ())), preferred_element_type=F32)


def dot_nt(a, b):
    return lax.dot_general(a, b, (((1,), (1,)), ((), ())), preferred_element_type=F32)


def iotas(shape):
    return lax.broadcasted_iota(jnp.int32, shape, 0), lax.broadcasted_iota(jnp.int32, shape, 1)


def core_index():
    return lax.rem(lax.axis_index("col"), 2)


def pack(gram, keep_ref, send_ref):
    i, j = iotas((H, H))
    low = gram[H:, H:]
    top = jnp.where(i >= j, gram[:H, :H], low)
    diag = jnp.sum(jnp.where(i == j, low, 0.0), axis=0, keepdims=True)
    tail = jnp.broadcast_to(diag, (8, H))
    core = core_index()

    def put(first_ref, second_ref):
        first_ref[0:H, :] = top
        first_ref[H:HALF, :] = tail
        second_ref[0:H, :] = gram[H:, :H]
        second_ref[H:HALF, :] = jnp.zeros((8, H), F32)

    @pl.when(core == 0)
    def _():
        put(keep_ref, send_ref)

    @pl.when(core == 1)
    def _():
        put(send_ref, keep_ref)


def unpack(mine_ref, other_ref, out_ref):
    core = core_index()
    i, j = iotas((H, H))

    def get(first_ref, second_ref):
        top = first_ref[0:H, :]
        topt = top.T
        diag = first_ref[H:H + 1, :]
        side = second_ref[0:H, :]
        out_ref[0:H, 0:H] = jnp.where(i >= j, top, topt)
        corner = jnp.where(i < j, top, topt)
        out_ref[H:, H:] = jnp.where(i == j, jnp.broadcast_to(diag, (H, H)), corner)
        out_ref[H:, 0:H] = side
        out_ref[0:H, H:] = side.T

    @pl.when(core == 0)
    def _():
        get(mine_ref, other_ref)

    @pl.when(core == 1)
    def _():
        get(other_ref, mine_ref)


def gram_kernel(steps, x_ref, keep_ref, send_ref, acc):
    step = pl.program_id(0)

    @pl.when(step == 0)
    def _():
        acc[...] = jnp.zeros_like(acc)

    h, m = split2(x_ref[...])
    acc[:, :2 * K] += dot_tn(h, jnp.concatenate([h, m], axis=1))
    acc[:, 2 * K:] += dot_tn(m, m)

    @pl.when(step == steps - 1)
    def _():
        cross = acc[:, K:2 * K]
        pack(acc[:, :K] + (cross + cross.T) + acc[:, 2 * K:], keep_ref, send_ref)


def gram_call(x, rows):
    steps = x.shape[0] // rows
    half = jax.ShapeDtypeStruct((HALF, H), F32)
    return pl.pallas_call(
        functools.partial(gram_kernel, steps),
        out_shape=(half, half),
        grid=(steps,),
        in_specs=[pl.BlockSpec((rows, K), lambda i: (i, 0))],
        out_specs=[VMEM_WHOLE] * 2,
        scratch_shapes=[pltpu.VMEM((K, 3 * K), F32)],
        compiler_params=params(58),
        name="gram_one",
    )(x)


def first_kernel(steps, x_ref, w_ref, first_ref, keep_ref, send_ref, acc):
    step = pl.program_id(0)

    @pl.when(step == 0)
    def _():
        acc[...] = jnp.zeros_like(acc)

    h, m, l = split3(x_ref[...])
    first = dot_nn(jnp.concatenate([h, m, l, h, m], axis=1), w_ref[...])
    first_ref[pl.ds(pl.multiple_of(step * x_ref.shape[0], x_ref.shape[0]), x_ref.shape[0]), :] = first
    fh, fm = split2(first)
    acc[...] += dot_tn(fh, jnp.concatenate([fh, fm], axis=1))

    @pl.when(step == steps - 1)
    def _():
        cross = acc[:, K:]
        pack(acc[:, :K] + (cross + cross.T), keep_ref, send_ref)


def first_call(x, w, rows):
    steps = x.shape[0] // rows
    half = jax.ShapeDtypeStruct((HALF, H), F32)
    return pl.pallas_call(
        functools.partial(first_kernel, steps),
        out_shape=(jax.ShapeDtypeStruct(x.shape, F32), half, half),
        grid=(steps,),
        in_specs=[pl.BlockSpec((rows, K), lambda i: (i, 0)), VMEM_WHOLE],
        out_specs=[VMEM_WHOLE] * 3,
        scratch_shapes=[pltpu.VMEM((K, 2 * K), F32)],
        compiler_params=params(30),
        name="first_and_gram_two",
    )(x, w)


def basis_kernel(scale, f_ref, c_ref, out_ref):
    rows = out_ref.shape[0]
    first = f_ref[pl.ds(pl.multiple_of(pl.program_id(0) * rows, rows), rows), :]
    h, m = split2(first)
    out_ref[...] = (first + dot_nn(jnp.concatenate([h, m, h], axis=1), c_ref[...])) * scale


def basis_call(first, c, rows, scale):
    return pl.pallas_call(
        functools.partial(basis_kernel, scale),
        out_shape=jax.ShapeDtypeStruct(first.shape, F32),
        grid=(first.shape[0] // rows,),
        in_specs=[VMEM_WHOLE] * 2,
        out_specs=pl.BlockSpec((rows, K), lambda i: (i, 0)),
        compiler_params=params(30),
        name="basis",
    )(first, c)


B = 32
S = 8


def eliminate(rows_a):
    rows_a = list(rows_a)
    width = rows_a[0].shape[1]
    sub = lax.broadcasted_iota(jnp.int32, (S, H), 0)
    for s in range(B // S):
        cols = [jnp.broadcast_to(rows_a[s][:, S * s + k:S * s + k + 1], (S, H)) for k in range(S)]
        x = rows_a[s]
        pivots, factors, us = [], [], []
        for j in range(S):
            r = jnp.broadcast_to(lax.rsqrt(cols[j][j:j + 1, :]), (S, H))
            lj = jnp.where(sub >= j, cols[j] * r, 0.0)
            fac = [None] * S
            for k in range(j + 1, S):
                fac[k] = jnp.broadcast_to(lj[k:k + 1, :], (S, H))
                cols[k] = cols[k] - lj * fac[k]
            u = jnp.broadcast_to(x[j:j + 1, :], (S, width)) * jnp.concatenate([r] * (width // H), axis=1)
            below = jnp.concatenate([jnp.where(sub > j, lj, 0.0)] * (width // H), axis=1)
            here = jnp.concatenate([sub == j] * (width // H), axis=1)
            x = jnp.where(here, u, x - below * u)
            pivots.append(r)
            factors.append(fac)
            us.append(u)
        rows_a[s] = x
        for q in range(s + 1, B // S):
            y = rows_a[q]
            c = [jnp.broadcast_to(y[:, S * s + k:S * s + k + 1], (S, H)) for k in range(S)]
            for j in range(S):
                lj = c[j] * pivots[j]
                for k in range(j + 1, S):
                    c[k] = c[k] - lj * factors[j][k]
                y = y - jnp.concatenate([lj] * (width // H), axis=1) * us[j]
            rows_a[q] = y
    return rows_a


def factorize(t_ref):
    def block(b, carry):
        r0 = pl.multiple_of(b * B, B)
        lane0 = pl.multiple_of(lax.div(b, H // B) * H, H)
        shift = lax.rem(b, H // B) * B
        d = t_ref[pl.ds(r0, B), pl.ds(lane0, H)]
        d = pltpu.roll(d, lax.rem(H - shift, H), 1)
        r = t_ref[pl.ds(r0, B), :]
        full = jnp.concatenate([d, r], axis=1)
        out = eliminate([full[S * s:S * s + S] for s in range(B // S)])
        u = jnp.concatenate([o[:, H:] for o in out], axis=0)
        t_ref[pl.ds(r0, B), :] = u
        lane = lax.broadcasted_iota(jnp.int32, (B, K), 1)
        left = jnp.where(lane >= r0 + B, u[:, :K], 0.0)
        lh, lm, ll = split3(left)
        uh, um, ul = split3(u)
        upd = dot_tn(
            jnp.concatenate([lh, lh, lm, lm, lh, ll], axis=0),
            jnp.concatenate([uh, um, uh, um, ul, uh], axis=0),
        )
        t_ref[...] -= upd
        return carry

    lax.fori_loop(0, K // B, block, 0)


def load_augmented(mine_ref, other_ref, t_ref):
    unpack(mine_ref, other_ref, t_ref.at[:, 0:K])
    i, j = iotas((K, K))
    t_ref[:, K:] = jnp.where(i == j, 1.0, 0.0)


def chol_one_kernel(mine_ref, other_ref, w_ref, upper_ref, t_ref):
    load_augmented(mine_ref, other_ref, t_ref)
    factorize(t_ref)
    i, j = iotas((K, K))
    upper_ref[...] = jnp.where(i <= j, t_ref[:, :K], 0.0)
    wt = jnp.where(i >= j, t_ref[:, K:], 0.0).T
    h, m = split2(wt)
    w_ref[0:K, :] = h
    w_ref[K:2 * K, :] = h
    w_ref[2 * K:3 * K, :] = h
    w_ref[3 * K:4 * K, :] = m
    w_ref[4 * K:5 * K, :] = m


def chol_one_call(mine, other):
    return pl.pallas_call(
        chol_one_kernel,
        out_shape=(jax.ShapeDtypeStruct((5 * K, K), BF16), jax.ShapeDtypeStruct((K, K), F32)),
        in_specs=[VMEM_WHOLE] * 2,
        out_specs=[VMEM_WHOLE] * 2,
        scratch_shapes=[pltpu.VMEM((K, 2 * K), F32)],
        compiler_params=params(16),
        name="factor_one",
    )(mine, other)


TOL = 1e-7


def largest(x):
    return jnp.max(jnp.abs(x))


def chol_two_kernel(scale, mine_ref, other_ref, upper_ref, c_ref, factor_ref, g_ref, x_ref, z_ref, t_ref):
    unpack(mine_ref, other_ref, g_ref)
    i, j = iotas((K, K))
    eye = jnp.where(i == j, 1.0, 0.0)
    half_low = jnp.where(i > j, 1.0, jnp.where(i == j, 0.5, 0.0))

    x_ref[...] = (g_ref[...] - eye) * half_low

    def x_more(state):
        step, change = state
        return jnp.logical_and(step < 10, jnp.logical_not(change <= TOL))

    def x_next(state):
        old = x_ref[...]
        h, m = split2(old)
        square = dot_nt(jnp.concatenate([h, h, m], axis=1), jnp.concatenate([h, m, h], axis=1))
        new = (g_ref[...] - eye - square) * half_low
        x_ref[...] = new
        return state[0] + 1, largest(new - old)

    _, change = lax.while_loop(x_more, x_next, (jnp.int32(0), jnp.float32(1.0)))
    x = x_ref[...]
    z_ref[...] = -x

    def residual():
        z = z_ref[...]
        xh, xm = split2(x_ref[...])
        zh, zm = split2(z)
        prod = dot_nn(jnp.concatenate([xh, xh, xm], axis=1), jnp.concatenate([zh, zm, zh], axis=0))
        return -(x_ref[...] + z + prod)

    def z_more(state):
        step, size = state
        return jnp.logical_and(step < 6, jnp.logical_not(size <= TOL))

    def z_next(state):
        r = residual()
        z = z_ref[...]
        rh, rm = split2(r)
        zh, zm = split2(z)
        z_ref[...] = z + r + dot_nn(jnp.concatenate([zh, zh, zm], axis=1), jnp.concatenate([rh, rm, rh], axis=0))
        return state[0] + 1, largest(r) * largest(r) * 256.0

    _, size = lax.while_loop(z_more, z_next, (jnp.int32(0), jnp.float32(1.0)))
    lowest = jnp.min(jnp.where(i == j, x, 0.0))
    good = jnp.logical_and(jnp.logical_and(change <= TOL, size <= TOL), lowest > -0.5)

    @pl.when(jnp.logical_not(good))
    def _():
        t_ref[:, :K] = g_ref[...]
        t_ref[:, K:] = eye
        factorize(t_ref)
        x_ref[...] = jnp.where(i <= j, t_ref[:, :K], 0.0).T - eye
        z_ref[...] = jnp.where(i >= j, t_ref[:, K:], 0.0) - eye

    ch, cm = split2(z_ref[...].T)
    c_ref[0:K, :] = ch
    c_ref[K:2 * K, :] = ch
    c_ref[2 * K:3 * K, :] = cm
    u1 = upper_ref[...]
    uh, um = split2(u1)
    xh, xm = split2(x_ref[...])
    prod = dot_tn(jnp.concatenate([xh, xh, xm], axis=0), jnp.concatenate([uh, um, uh], axis=0))
    factor_ref[...] = (u1 + prod) / scale


def chol_two_call(mine, other, upper, scale):
    return pl.pallas_call(
        functools.partial(chol_two_kernel, scale),
        out_shape=(jax.ShapeDtypeStruct((3 * K, K), BF16), jax.ShapeDtypeStruct((K, K), F32)),
        in_specs=[VMEM_WHOLE] * 3,
        out_specs=[VMEM_WHOLE] * 2,
        scratch_shapes=[pltpu.VMEM((K, K), F32)] * 3 + [pltpu.VMEM((K, 2 * K), F32)],
        compiler_params=params(16),
        name="factor_two",
    )(mine, other, upper)


def swap(value, axis, distance):
    return lax.ppermute(value, axis, [(i, i ^ distance) for i in range(lax.axis_size(axis))])


def sum_over(value, axis, step):
    a, b, c = [swap(value, axis, step * d) for d in (1, 2, 3)]
    return (value + a) + (b + c)


def reduce_gram(keep, send):
    value = keep + swap(send, "col", 1)
    value = sum_over(value, "col", 2)
    value = sum_over(value, "row", 1)
    value = sum_over(value, "row", 4)
    return value, swap(value, "col", 1)


ROWS_PER_STEP = 2048


def shards(panel):
    total_rows = panel.shape[0] * lax.axis_size("row") * lax.axis_size("col")
    scale = float(total_rows) ** 0.5
    mine, other = reduce_gram(*gram_call(panel, ROWS_PER_STEP))
    w, upper = chol_one_call(mine, other)
    first, keep, send = first_call(panel, w, ROWS_PER_STEP)
    mine, other = reduce_gram(keep, send)
    c, factor = chol_two_call(mine, other, upper, scale)
    return basis_call(first, c, ROWS_PER_STEP, scale), factor


def solution(mesh):
    return jax.shard_map(
        shards,
        mesh=mesh,
        in_specs=(P(("row", "col"), None),),
        out_specs=(P(("row", "col"), None), P()),
        check_vma=False,
    )
```

```python
import functools
import jax
import jax.numpy as jnp
from jax import lax
from jax.experimental import pallas as pl
from jax.experimental.pallas import tpu as pltpu
from jax.sharding import PartitionSpec as P

K = 256
H = 128
HALF = 136
F32 = jnp.float32
BF16 = jnp.bfloat16
VMEM_WHOLE = pl.BlockSpec(memory_space=pltpu.VMEM)


def params(mib):
    return pltpu.CompilerParams(vmem_limit_bytes=mib << 20)


def split2(x):
    hi = x.astype(BF16)
    return hi, (x - hi.astype(F32)).astype(BF16)


def split3(x):
    hi = x.astype(BF16)
    rest = x - hi.astype(F32)
    mid = rest.astype(BF16)
    return hi, mid, (rest - mid.astype(F32)).astype(BF16)


def dot_tn(a, b):
    return lax.dot_general(a, b, (((0,), (0,)), ((), ())), preferred_element_type=F32)


def dot_nn(a, b):
    return lax.dot_general(a, b, (((1,), (0,)), ((), ())), preferred_element_type=F32)


def dot_nt(a, b):
    return lax.dot_general(a, b, (((1,), (1,)), ((), ())), preferred_element_type=F32)


def iotas(shape):
    return lax.broadcasted_iota(jnp.int32, shape, 0), lax.broadcasted_iota(jnp.int32, shape, 1)


def core_index():
    return lax.rem(lax.axis_index("col"), 2)


def pack(gram, keep_ref, send_ref):
    i, j = iotas((H, H))
    low = gram[H:, H:]
    top = jnp.where(i >= j, gram[:H, :H], low)
    diag = jnp.sum(jnp.where(i == j, low, 0.0), axis=0, keepdims=True)
    tail = jnp.broadcast_to(diag, (8, H))
    core = core_index()

    def put(first_ref, second_ref):
        first_ref[0:H, :] = top
        first_ref[H:HALF, :] = tail
        second_ref[0:H, :] = gram[H:, :H]
        second_ref[H:HALF, :] = jnp.zeros((8, H), F32)

    @pl.when(core == 0)
    def _():
        put(keep_ref, send_ref)

    @pl.when(core == 1)
    def _():
        put(send_ref, keep_ref)


def unpack(mine_ref, other_ref, out_ref):
    core = core_index()
    i, j = iotas((H, H))

    def get(first_ref, second_ref):
        top = first_ref[0:H, :]
        topt = top.T
        diag = first_ref[H:H + 1, :]
        side = second_ref[0:H, :]
        out_ref[0:H, 0:H] = jnp.where(i >= j, top, topt)
        corner = jnp.where(i < j, top, topt)
        out_ref[H:, H:] = jnp.where(i == j, jnp.broadcast_to(diag, (H, H)), corner)
        out_ref[H:, 0:H] = side
        out_ref[0:H, H:] = side.T

    @pl.when(core == 0)
    def _():
        get(mine_ref, other_ref)

    @pl.when(core == 1)
    def _():
        get(other_ref, mine_ref)


def gram_kernel(rows, x_hbm, keep_ref, send_ref, x_ref, acc, sems):
    steps = x_hbm.shape[0] // rows

    def part(step):
        return pl.ds(pl.multiple_of(step * rows, rows), rows)

    def copy(step):
        return pltpu.make_async_copy(x_hbm.at[part(step)], x_ref.at[part(step)], sems.at[step])

    for step in range(steps):
        copy(step).start()
    acc[...] = jnp.zeros_like(acc)

    def body(step, carry):
        copy(step).wait()
        h, m = split2(x_ref[part(step), :])
        acc[:, : 2 * K] += dot_tn(h, jnp.concatenate([h, m], axis=1))
        acc[:, 2 * K :] += dot_tn(m, m)
        return carry

    lax.fori_loop(0, steps, body, 0)
    cross = acc[:, K : 2 * K]
    pack(acc[:, :K] + (cross + cross.T) + acc[:, 2 * K :], keep_ref, send_ref)


def gram_call(x, rows):
    half = jax.ShapeDtypeStruct((HALF, H), F32)
    return pl.pallas_call(
        functools.partial(gram_kernel, rows),
        out_shape=(half, half),
        in_specs=[pl.BlockSpec(memory_space=pltpu.HBM)],
        out_specs=[VMEM_WHOLE] * 2,
        scratch_shapes=[
            pltpu.VMEM(x.shape, F32),
            pltpu.VMEM((K, 3 * K), F32),
            pltpu.SemaphoreType.DMA((x.shape[0] // rows,)),
        ],
        compiler_params=params(52),
        name="gram_one",
    )(x)


def first_kernel(rows, x_hbm, w_ref, first_ref, keep_ref, send_ref, x_ref, acc, sems):
    steps = x_hbm.shape[0] // rows

    def copy(step):
        part = pl.ds(pl.multiple_of(step * rows, rows), rows)
        return pltpu.make_async_copy(x_hbm.at[part], x_ref.at[part], sems.at[step])

    for step in range(steps):
        copy(step).start()
    acc[...] = jnp.zeros_like(acc)

    def body(step, carry):
        copy(step).wait()
        total = None
        for n in range(2):
            part = pl.ds(pl.multiple_of(step * rows + n * (rows // 2), rows // 2), rows // 2)
            h, m, l = split3(x_ref[part, :])
            upper = jnp.concatenate([h[:, :H], m[:, :H], h[:, :H], m[:, :H], l], axis=1)
            lower = jnp.concatenate([h[:, H:], m[:, H:]], axis=1)
            first = dot_nn(upper, w_ref[: 3 * K, :])
            more = dot_nn(lower, w_ref[3 * K :, :])
            first = jnp.concatenate([first[:, :H], first[:, H:] + (more[:, :H] + more[:, H:])], axis=1)
            first_ref[part, :] = first
            fh, fm = split2(first)
            gram = dot_tn(fh, jnp.concatenate([fh, fm], axis=1))
            total = gram if total is None else total + gram
        acc[...] += total
        return carry

    lax.fori_loop(0, steps, body, 0)
    cross = acc[:, K:]
    pack(acc[:, :K] + (cross + cross.T), keep_ref, send_ref)


def first_call(x, w, rows):
    half = jax.ShapeDtypeStruct((HALF, H), F32)
    return pl.pallas_call(
        functools.partial(first_kernel, rows),
        out_shape=(jax.ShapeDtypeStruct(x.shape, F32), half, half),
        in_specs=[pl.BlockSpec(memory_space=pltpu.HBM), VMEM_WHOLE],
        out_specs=[VMEM_WHOLE] * 3,
        scratch_shapes=[
            pltpu.VMEM(x.shape, F32),
            pltpu.VMEM((K, 2 * K), F32),
            pltpu.SemaphoreType.DMA((x.shape[0] // rows,)),
        ],
        compiler_params=params(36),
        name="first_and_gram_two",
    )(x, w)


def basis_kernel(scale, small_ref, f_ref, c_ref, out_ref):
    rows = out_ref.shape[0]
    first = f_ref[pl.ds(pl.multiple_of(pl.program_id(0) * rows, rows), rows), :]

    @pl.when(small_ref[0] == 1)
    def _():
        out_ref[...] = (first + dot_nn(first.astype(BF16), c_ref[:K, :])) * scale

    @pl.when(small_ref[0] == 0)
    def _():
        h, m = split2(first)
        out_ref[...] = (first + dot_nn(jnp.concatenate([h, m, h], axis=1), c_ref[...])) * scale


def basis_call(small, first, c, rows, scale):
    return pl.pallas_call(
        functools.partial(basis_kernel, scale),
        out_shape=jax.ShapeDtypeStruct(first.shape, F32),
        grid=(first.shape[0] // rows,),
        in_specs=[pl.BlockSpec(memory_space=pltpu.SMEM)] + [VMEM_WHOLE] * 2,
        out_specs=pl.BlockSpec((rows, K), lambda i: (i, 0)),
        compiler_params=params(30),
        name="basis",
    )(small, first, c)


B = 32
S = 8


def eliminate(rows_a):
    rows_a = list(rows_a)
    width = rows_a[0].shape[1]
    sub = lax.broadcasted_iota(jnp.int32, (S, H), 0)
    for s in range(B // S):
        cols = [jnp.broadcast_to(rows_a[s][:, S * s + k:S * s + k + 1], (S, H)) for k in range(S)]
        x = rows_a[s]
        pivots, factors, us = [], [], []
        for j in range(S):
            r = jnp.broadcast_to(lax.rsqrt(cols[j][j:j + 1, :]), (S, H))
            lj = jnp.where(sub >= j, cols[j] * r, 0.0)
            fac = [None] * S
            for k in range(j + 1, S):
                fac[k] = jnp.broadcast_to(lj[k:k + 1, :], (S, H))
                cols[k] = cols[k] - lj * fac[k]
            u = jnp.broadcast_to(x[j:j + 1, :], (S, width)) * jnp.concatenate([r] * (width // H), axis=1)
            below = jnp.concatenate([jnp.where(sub > j, lj, 0.0)] * (width // H), axis=1)
            here = jnp.concatenate([sub == j] * (width // H), axis=1)
            x = jnp.where(here, u, x - below * u)
            pivots.append(r)
            factors.append(fac)
            us.append(u)
        rows_a[s] = x
        for q in range(s + 1, B // S):
            y = rows_a[q]
            c = [jnp.broadcast_to(y[:, S * s + k:S * s + k + 1], (S, H)) for k in range(S)]
            for j in range(S):
                lj = c[j] * pivots[j]
                for k in range(j + 1, S):
                    c[k] = c[k] - lj * factors[j][k]
                y = y - jnp.concatenate([lj] * (width // H), axis=1) * us[j]
            rows_a[q] = y
    return rows_a


def factorize(t_ref):
    def block(b, carry):
        r0 = pl.multiple_of(b * B, B)
        lane0 = pl.multiple_of(lax.div(b, H // B) * H, H)
        shift = lax.rem(b, H // B) * B
        d = t_ref[pl.ds(r0, B), pl.ds(lane0, H)]
        d = pltpu.roll(d, lax.rem(H - shift, H), 1)
        r = t_ref[pl.ds(r0, B), :]
        full = jnp.concatenate([d, r], axis=1)
        out = eliminate([full[S * s:S * s + S] for s in range(B // S)])
        u = jnp.concatenate([o[:, H:] for o in out], axis=0)
        t_ref[pl.ds(r0, B), :] = u
        lane = lax.broadcasted_iota(jnp.int32, (B, K), 1)
        left = jnp.where(lane >= r0 + B, u[:, :K], 0.0)
        lh, lm, ll = split3(left)
        uh, um, ul = split3(u)
        upd = dot_tn(
            jnp.concatenate([lh, lh, lm, lm, lh, ll], axis=0),
            jnp.concatenate([uh, um, uh, um, ul, uh], axis=0),
        )
        t_ref[...] -= upd
        return carry

    lax.fori_loop(0, K // B, block, 0)


def chol_one_kernel(mine_ref, other_ref, w_ref, upper_ref, t_ref):
    unpack(mine_ref, other_ref, t_ref.at[:, 0:K])
    i, j = iotas((K, K))
    t_ref[:, K:] = jnp.where(i == j, 1.0, 0.0)
    factorize(t_ref)
    upper_ref[...] = jnp.where(i <= j, t_ref[:, :K], 0.0)
    h, m = split2(jnp.where(i >= j, t_ref[:, K:], 0.0).T)
    for n in range(2):
        w_ref[n * H : (n + 1) * H, :] = h[:H]
        w_ref[(2 + n) * H : (3 + n) * H, :] = m[:H]
        w_ref[(6 + n) * H : (7 + n) * H, :] = jnp.concatenate([h[H:, H:], m[H:, H:]], axis=1)
    w_ref[2 * K : 3 * K, :] = h


def chol_one_call(mine, other):
    return pl.pallas_call(
        chol_one_kernel,
        out_shape=(jax.ShapeDtypeStruct((4 * K, K), BF16), jax.ShapeDtypeStruct((K, K), F32)),
        in_specs=[VMEM_WHOLE] * 2,
        out_specs=[VMEM_WHOLE] * 2,
        scratch_shapes=[pltpu.VMEM((K, 2 * K), F32)],
        compiler_params=params(16),
        name="factor_one",
    )(mine, other)


TOL = 1e-7
SMALL = 4e-3


def largest(x):
    return jnp.max(jnp.abs(x))


def chol_two_kernel(scale, mine_ref, other_ref, upper_ref, small_ref, c_ref, factor_ref, g_ref, x_ref, z_ref, t_ref):
    unpack(mine_ref, other_ref, g_ref)
    i, j = iotas((K, K))
    eye = jnp.where(i == j, 1.0, 0.0)
    half_low = jnp.where(i > j, 1.0, jnp.where(i == j, 0.5, 0.0))

    x_ref[...] = (g_ref[...] - eye) * half_low

    def x_more(state):
        step, change = state
        return jnp.logical_and(step < 10, jnp.logical_not(change <= TOL))

    def x_next(state):
        old = x_ref[...]
        h, m = split2(old)
        square = dot_nt(jnp.concatenate([h, h, m], axis=1), jnp.concatenate([h, m, h], axis=1))
        new = (g_ref[...] - eye - square) * half_low
        x_ref[...] = new
        return state[0] + 1, largest(new - old)

    _, change = lax.while_loop(x_more, x_next, (jnp.int32(0), jnp.float32(1.0)))
    x = x_ref[...]
    z_ref[...] = -x

    def residual():
        z = z_ref[...]
        xh, xm = split2(x_ref[...])
        zh, zm = split2(z)
        prod = dot_nn(jnp.concatenate([xh, xh, xm], axis=1), jnp.concatenate([zh, zm, zh], axis=0))
        return -(x_ref[...] + z + prod)

    def z_more(state):
        step, size = state
        return jnp.logical_and(step < 6, jnp.logical_not(size <= TOL))

    def z_next(state):
        r = residual()
        z = z_ref[...]
        rh, rm = split2(r)
        zh, zm = split2(z)
        z_ref[...] = z + r + dot_nn(jnp.concatenate([zh, zh, zm], axis=1), jnp.concatenate([rh, rm, rh], axis=0))
        return state[0] + 1, largest(r) * largest(r) * 256.0

    _, size = lax.while_loop(z_more, z_next, (jnp.int32(0), jnp.float32(1.0)))
    lowest = jnp.min(jnp.where(i == j, x, 0.0))
    good = jnp.logical_and(jnp.logical_and(change <= TOL, size <= TOL), lowest > -0.5)

    @pl.when(jnp.logical_not(good))
    def _():
        t_ref[:, :K] = g_ref[...]
        t_ref[:, K:] = eye
        factorize(t_ref)
        x_ref[...] = jnp.where(i <= j, t_ref[:, :K], 0.0).T - eye
        z_ref[...] = jnp.where(i >= j, t_ref[:, K:], 0.0) - eye

    z = z_ref[...]
    small_ref[0] = (jnp.sum(z * z) <= SMALL * SMALL * K).astype(jnp.int32)
    ch, cm = split2(z.T)
    c_ref[0:K, :] = ch
    c_ref[K:2 * K, :] = ch
    c_ref[2 * K:3 * K, :] = cm
    u1 = upper_ref[...]
    uh, um = split2(u1)
    xh, xm = split2(x_ref[...])
    prod = dot_tn(jnp.concatenate([xh, xh, xm], axis=0), jnp.concatenate([uh, um, uh], axis=0))
    factor_ref[...] = (u1 + prod) / scale


def chol_two_call(mine, other, upper, scale):
    return pl.pallas_call(
        functools.partial(chol_two_kernel, scale),
        out_shape=(
            jax.ShapeDtypeStruct((1,), jnp.int32),
            jax.ShapeDtypeStruct((3 * K, K), BF16),
            jax.ShapeDtypeStruct((K, K), F32),
        ),
        in_specs=[VMEM_WHOLE] * 3,
        out_specs=[pl.BlockSpec(memory_space=pltpu.SMEM)] + [VMEM_WHOLE] * 2,
        scratch_shapes=[pltpu.VMEM((K, K), F32)] * 3 + [pltpu.VMEM((K, 2 * K), F32)],
        compiler_params=params(16),
        name="factor_two",
    )(mine, other, upper)


def swap(value, axis, distance):
    return lax.ppermute(value, axis, [(i, i ^ distance) for i in range(lax.axis_size(axis))])


def sum_over(value, axis, step):
    a, b, c = [swap(value, axis, step * d) for d in (1, 2, 3)]
    return (value + a) + (b + c)


def reduce_gram(keep, send):
    value = keep + swap(send, "col", 1)
    value = sum_over(value, "col", 2)
    value = sum_over(value, "row", 1)
    value = sum_over(value, "row", 4)
    return value, swap(value, "col", 1)


ROWS_PER_STEP = 2048
FIRST_ROWS_PER_STEP = 3072


def shards(panel):
    total_rows = panel.shape[0] * lax.axis_size("row") * lax.axis_size("col")
    scale = float(total_rows) ** 0.5
    keep, send = gram_call(panel, ROWS_PER_STEP)
    w, upper = chol_one_call(*reduce_gram(keep, send))
    first, keep, send = first_call(panel, w, FIRST_ROWS_PER_STEP)
    small, c, factor = chol_two_call(*reduce_gram(keep, send), upper, scale)
    return basis_call(small, first, c, ROWS_PER_STEP, scale), factor


def solution(mesh):
    return jax.shard_map(
        shards,
        mesh=mesh,
        in_specs=(P(("row", "col"), None),),
        out_specs=(P(("row", "col"), None), P()),
        check_vma=False,
    )
```

```python
import functools
import jax
import jax.numpy as jnp
from jax import lax
from jax.experimental import pallas as pl
from jax.experimental.pallas import tpu as pltpu
from jax.sharding import PartitionSpec as P

K = 256
H = 128
HALF = 136
F32 = jnp.float32
BF16 = jnp.bfloat16
VMEM_WHOLE = pl.BlockSpec(memory_space=pltpu.VMEM)


def params(mib):
    return pltpu.CompilerParams(vmem_limit_bytes=mib << 20)


def split2(x):
    hi = x.astype(BF16)
    return hi, (x - hi.astype(F32)).astype(BF16)


def split3(x):
    hi = x.astype(BF16)
    rest = x - hi.astype(F32)
    mid = rest.astype(BF16)
    return hi, mid, (rest - mid.astype(F32)).astype(BF16)


def dot_tn(a, b):
    return lax.dot_general(a, b, (((0,), (0,)), ((), ())), preferred_element_type=F32)


def dot_nn(a, b):
    return lax.dot_general(a, b, (((1,), (0,)), ((), ())), preferred_element_type=F32)


def dot_nt(a, b):
    return lax.dot_general(a, b, (((1,), (1,)), ((), ())), preferred_element_type=F32)


def iotas(shape):
    return lax.broadcasted_iota(jnp.int32, shape, 0), lax.broadcasted_iota(jnp.int32, shape, 1)


def core_index():
    return lax.rem(lax.axis_index("col"), 2)


def pack(gram, keep_ref, send_ref):
    i, j = iotas((H, H))
    low = gram[H:, H:]
    top = jnp.where(i >= j, gram[:H, :H], low)
    diag = jnp.sum(jnp.where(i == j, low, 0.0), axis=0, keepdims=True)
    tail = jnp.broadcast_to(diag, (8, H))
    core = core_index()

    def put(first_ref, second_ref):
        first_ref[0:H, :] = top
        first_ref[H:HALF, :] = tail
        second_ref[0:H, :] = gram[H:, :H]
        second_ref[H:HALF, :] = jnp.zeros((8, H), F32)

    @pl.when(core == 0)
    def _():
        put(keep_ref, send_ref)

    @pl.when(core == 1)
    def _():
        put(send_ref, keep_ref)


def unpack(mine_ref, other_ref, out_ref):
    core = core_index()
    i, j = iotas((H, H))

    def get(first_ref, second_ref):
        top = first_ref[0:H, :]
        topt = top.T
        diag = first_ref[H:H + 1, :]
        side = second_ref[0:H, :]
        out_ref[0:H, 0:H] = jnp.where(i >= j, top, topt)
        corner = jnp.where(i < j, top, topt)
        out_ref[H:, H:] = jnp.where(i == j, jnp.broadcast_to(diag, (H, H)), corner)
        out_ref[H:, 0:H] = side
        out_ref[0:H, H:] = side.T

    @pl.when(core == 0)
    def _():
        get(mine_ref, other_ref)

    @pl.when(core == 1)
    def _():
        get(other_ref, mine_ref)


def gram_kernel(rows, x_hbm, keep_ref, send_ref, x_ref, acc, sems):
    steps = x_hbm.shape[0] // rows

    def part(step):
        return pl.ds(pl.multiple_of(step * rows, rows), rows)

    def copy(step):
        return pltpu.make_async_copy(x_hbm.at[part(step)], x_ref.at[part(step)], sems.at[step])

    for step in range(steps):
        copy(step).start()
    acc[...] = jnp.zeros_like(acc)

    def body(step, carry):
        copy(step).wait()
        h, m = split2(x_ref[part(step), :])
        acc[:, : 2 * K] += dot_tn(h, jnp.concatenate([h, m], axis=1))
        acc[:, 2 * K :] += dot_tn(m, m)
        return carry

    lax.fori_loop(0, steps, body, 0)
    cross = acc[:, K : 2 * K]
    pack(acc[:, :K] + (cross + cross.T) + acc[:, 2 * K :], keep_ref, send_ref)


def gram_call(x, rows):
    half = jax.ShapeDtypeStruct((HALF, H), F32)
    return pl.pallas_call(
        functools.partial(gram_kernel, rows),
        out_shape=(half, half),
        in_specs=[pl.BlockSpec(memory_space=pltpu.HBM)],
        out_specs=[VMEM_WHOLE] * 2,
        scratch_shapes=[
            pltpu.VMEM(x.shape, F32),
            pltpu.VMEM((K, 3 * K), F32),
            pltpu.SemaphoreType.DMA((x.shape[0] // rows,)),
        ],
        compiler_params=params(52),
        name="gram_one",
    )(x)


def first_kernel(rows, x_hbm, w_ref, first_ref, keep_ref, send_ref, x_ref, acc, sems):
    steps = x_hbm.shape[0] // rows

    def copy(step):
        part = pl.ds(pl.multiple_of(step * rows, rows), rows)
        return pltpu.make_async_copy(x_hbm.at[part], x_ref.at[part], sems.at[step])

    for step in range(steps):
        copy(step).start()
    acc[...] = jnp.zeros_like(acc)

    def body(step, carry):
        copy(step).wait()
        total = None
        for n in range(2):
            part = pl.ds(pl.multiple_of(step * rows + n * (rows // 2), rows // 2), rows // 2)
            h, m, l = split3(x_ref[part, :])
            upper = jnp.concatenate([h[:, :H], m[:, :H], h[:, :H], m[:, :H], l], axis=1)
            lower = jnp.concatenate([h[:, H:], m[:, H:]], axis=1)
            first = dot_nn(upper, w_ref[: 3 * K, :])
            more = dot_nn(lower, w_ref[3 * K :, :])
            first = jnp.concatenate([first[:, :H], first[:, H:] + (more[:, :H] + more[:, H:])], axis=1)
            first_ref[part, :] = first
            fh, fm = split2(first)
            gram = dot_tn(fh, jnp.concatenate([fh, fm], axis=1))
            total = gram if total is None else total + gram
        acc[...] += total
        return carry

    lax.fori_loop(0, steps, body, 0)
    cross = acc[:, K:]
    pack(acc[:, :K] + (cross + cross.T), keep_ref, send_ref)


def first_call(x, w, rows):
    half = jax.ShapeDtypeStruct((HALF, H), F32)
    return pl.pallas_call(
        functools.partial(first_kernel, rows),
        out_shape=(jax.ShapeDtypeStruct(x.shape, F32), half, half),
        in_specs=[pl.BlockSpec(memory_space=pltpu.HBM), VMEM_WHOLE],
        out_specs=[VMEM_WHOLE] * 3,
        scratch_shapes=[
            pltpu.VMEM(x.shape, F32),
            pltpu.VMEM((K, 2 * K), F32),
            pltpu.SemaphoreType.DMA((x.shape[0] // rows,)),
        ],
        compiler_params=params(36),
        name="first_and_gram_two",
    )(x, w)


def basis_kernel(rows, scale, small_ref, f_ref, c_ref, out_hbm, out_ref, sems):
    steps = f_ref.shape[0] // rows

    def part(step):
        return pl.ds(pl.multiple_of(step * rows, rows), rows)

    def copy(step):
        return pltpu.make_async_copy(out_ref.at[part(step)], out_hbm.at[part(step)], sems.at[step])

    def run(correction):
        def body(step, carry):
            first = f_ref[part(step), :]
            out_ref[part(step), :] = (first + correction(first)) * scale
            copy(step).start()
            return carry

        lax.fori_loop(0, steps, body, 0)

    def one_product(first):
        return dot_nn(first.astype(BF16), c_ref[:K, :])

    def three_products(first):
        h, m = split2(first)
        return dot_nn(jnp.concatenate([h, m, h], axis=1), c_ref[...])

    @pl.when(small_ref[0] == 1)
    def _():
        run(one_product)

    @pl.when(small_ref[0] == 0)
    def _():
        run(three_products)

    for step in range(steps):
        copy(step).wait()


def basis_call(small, first, c, rows, scale):
    return pl.pallas_call(
        functools.partial(basis_kernel, rows, scale),
        out_shape=jax.ShapeDtypeStruct(first.shape, F32),
        in_specs=[pl.BlockSpec(memory_space=pltpu.SMEM)] + [VMEM_WHOLE] * 2,
        out_specs=pl.BlockSpec(memory_space=pltpu.HBM),
        scratch_shapes=[pltpu.VMEM(first.shape, F32), pltpu.SemaphoreType.DMA((first.shape[0] // rows,))],
        compiler_params=params(34),
        name="basis",
    )(small, first, c)


B = 32
S = 8


def eliminate(rows_a):
    rows_a = list(rows_a)
    width = rows_a[0].shape[1]
    sub = lax.broadcasted_iota(jnp.int32, (S, H), 0)
    for s in range(B // S):
        cols = [jnp.broadcast_to(rows_a[s][:, S * s + k:S * s + k + 1], (S, H)) for k in range(S)]
        x = rows_a[s]
        pivots, factors, us = [], [], []
        for j in range(S):
            r = jnp.broadcast_to(lax.rsqrt(cols[j][j:j + 1, :]), (S, H))
            lj = jnp.where(sub >= j, cols[j] * r, 0.0)
            fac = [None] * S
            for k in range(j + 1, S):
                fac[k] = jnp.broadcast_to(lj[k:k + 1, :], (S, H))
                cols[k] = cols[k] - lj * fac[k]
            u = jnp.broadcast_to(x[j:j + 1, :], (S, width)) * jnp.concatenate([r] * (width // H), axis=1)
            below = jnp.concatenate([jnp.where(sub > j, lj, 0.0)] * (width // H), axis=1)
            here = jnp.concatenate([sub == j] * (width // H), axis=1)
            x = jnp.where(here, u, x - below * u)
            pivots.append(r)
            factors.append(fac)
            us.append(u)
        rows_a[s] = x
        for q in range(s + 1, B // S):
            y = rows_a[q]
            c = [jnp.broadcast_to(y[:, S * s + k:S * s + k + 1], (S, H)) for k in range(S)]
            for j in range(S):
                lj = c[j] * pivots[j]
                for k in range(j + 1, S):
                    c[k] = c[k] - lj * factors[j][k]
                y = y - jnp.concatenate([lj] * (width // H), axis=1) * us[j]
            rows_a[q] = y
    return rows_a


def factorize(t_ref):
    for side in range(2):
        lanes = slice(side * H, side * H + 3 * H)
        below = slice(side * H, K)
        width = K - side * H

        def block(b, carry):
            r0 = pl.multiple_of(b * B, B)
            shift = r0 - side * H
            r = t_ref[pl.ds(r0, B), lanes]
            d = pltpu.roll(r[:, :H], lax.rem(H - shift, H), 1)
            full = jnp.concatenate([d, r], axis=1)
            out = eliminate([full[S * s : S * s + S] for s in range(B // S)])
            u = jnp.concatenate([o[:, H:] for o in out], axis=0)
            t_ref[pl.ds(r0, B), lanes] = u
            lane = lax.broadcasted_iota(jnp.int32, (B, width), 1)
            left = jnp.where(lane >= shift + B, u[:, :width], 0.0)
            lh, lm, ll = split3(left)
            uh, um, ul = split3(u)
            t_ref[below, lanes] -= dot_tn(
                jnp.concatenate([lh, lh, lm, lm, lh, ll], axis=0),
                jnp.concatenate([uh, um, uh, um, ul, uh], axis=0),
            )
            return carry

        lax.fori_loop(side * (H // B), (side + 1) * (H // B), block, 0)


def chol_one_kernel(mine_ref, other_ref, w_ref, upper_ref, t_ref):
    unpack(mine_ref, other_ref, t_ref.at[:, 0:K])
    i, j = iotas((K, K))
    t_ref[:, K:] = jnp.where(i == j, 1.0, 0.0)
    factorize(t_ref)
    upper_ref[...] = jnp.where(i <= j, t_ref[:, :K], 0.0)
    h, m = split2(jnp.where(i >= j, t_ref[:, K:], 0.0).T)
    for n in range(2):
        w_ref[n * H : (n + 1) * H, :] = h[:H]
        w_ref[(2 + n) * H : (3 + n) * H, :] = m[:H]
        w_ref[(6 + n) * H : (7 + n) * H, :] = jnp.concatenate([h[H:, H:], m[H:, H:]], axis=1)
    w_ref[2 * K : 3 * K, :] = h


def chol_one_call(mine, other):
    return pl.pallas_call(
        chol_one_kernel,
        out_shape=(jax.ShapeDtypeStruct((4 * K, K), BF16), jax.ShapeDtypeStruct((K, K), F32)),
        in_specs=[VMEM_WHOLE] * 2,
        out_specs=[VMEM_WHOLE] * 2,
        scratch_shapes=[pltpu.VMEM((K, 2 * K), F32)],
        compiler_params=params(16),
        name="factor_one",
    )(mine, other)


TOL = 1e-7
SMALL = 4e-3


def largest(x):
    return jnp.max(jnp.abs(x))


def chol_two_kernel(scale, mine_ref, other_ref, upper_ref, small_ref, c_ref, factor_ref, g_ref, x_ref, z_ref, t_ref):
    unpack(mine_ref, other_ref, g_ref)
    i, j = iotas((K, K))
    eye = jnp.where(i == j, 1.0, 0.0)
    half_low = jnp.where(i > j, 1.0, jnp.where(i == j, 0.5, 0.0))

    x_ref[...] = (g_ref[...] - eye) * half_low

    def x_more(state):
        step, change = state
        return jnp.logical_and(step < 10, jnp.logical_not(change <= TOL))

    def x_next(state):
        old = x_ref[...]
        h, m = split2(old)
        square = dot_nt(jnp.concatenate([h, h, m], axis=1), jnp.concatenate([h, m, h], axis=1))
        new = (g_ref[...] - eye - square) * half_low
        x_ref[...] = new
        return state[0] + 1, largest(new - old)

    _, change = lax.while_loop(x_more, x_next, (jnp.int32(0), jnp.float32(1.0)))
    x = x_ref[...]
    z_ref[...] = -x

    def residual():
        z = z_ref[...]
        xh, xm = split2(x_ref[...])
        zh, zm = split2(z)
        prod = dot_nn(jnp.concatenate([xh, xh, xm], axis=1), jnp.concatenate([zh, zm, zh], axis=0))
        return -(x_ref[...] + z + prod)

    def z_more(state):
        step, size = state
        return jnp.logical_and(step < 6, jnp.logical_not(size <= TOL))

    def z_next(state):
        r = residual()
        z = z_ref[...]
        rh, rm = split2(r)
        zh, zm = split2(z)
        z_ref[...] = z + r + dot_nn(jnp.concatenate([zh, zh, zm], axis=1), jnp.concatenate([rh, rm, rh], axis=0))
        return state[0] + 1, largest(r) * largest(r) * 256.0

    _, size = lax.while_loop(z_more, z_next, (jnp.int32(0), jnp.float32(1.0)))
    lowest = jnp.min(jnp.where(i == j, x, 0.0))
    good = jnp.logical_and(jnp.logical_and(change <= TOL, size <= TOL), lowest > -0.5)

    @pl.when(jnp.logical_not(good))
    def _():
        t_ref[:, :K] = g_ref[...]
        t_ref[:, K:] = eye
        factorize(t_ref)
        x_ref[...] = jnp.where(i <= j, t_ref[:, :K], 0.0).T - eye
        z_ref[...] = jnp.where(i >= j, t_ref[:, K:], 0.0) - eye

    z = z_ref[...]
    small_ref[0] = (jnp.sum(z * z) <= SMALL * SMALL * K).astype(jnp.int32)
    ch, cm = split2(z.T)
    c_ref[0:K, :] = ch
    c_ref[K:2 * K, :] = ch
    c_ref[2 * K:3 * K, :] = cm
    u1 = upper_ref[...]
    uh, um = split2(u1)
    xh, xm = split2(x_ref[...])
    prod = dot_tn(jnp.concatenate([xh, xh, xm], axis=0), jnp.concatenate([uh, um, uh], axis=0))
    factor_ref[...] = (u1 + prod) / scale


def chol_two_call(mine, other, upper, scale):
    return pl.pallas_call(
        functools.partial(chol_two_kernel, scale),
        out_shape=(
            jax.ShapeDtypeStruct((1,), jnp.int32),
            jax.ShapeDtypeStruct((3 * K, K), BF16),
            jax.ShapeDtypeStruct((K, K), F32),
        ),
        in_specs=[VMEM_WHOLE] * 3,
        out_specs=[pl.BlockSpec(memory_space=pltpu.SMEM)] + [VMEM_WHOLE] * 2,
        scratch_shapes=[pltpu.VMEM((K, K), F32)] * 3 + [pltpu.VMEM((K, 2 * K), F32)],
        compiler_params=params(16),
        name="factor_two",
    )(mine, other, upper)


def swap(value, axis, distance):
    return lax.ppermute(value, axis, [(i, i ^ distance) for i in range(lax.axis_size(axis))])


def sum_over(value, axis, step):
    a, b, c = [swap(value, axis, step * d) for d in (1, 2, 3)]
    return (value + a) + (b + c)


def reduce_gram(keep, send):
    value = keep + swap(send, "col", 1)
    value = sum_over(value, "col", 2)
    value = sum_over(value, "row", 1)
    value = sum_over(value, "row", 4)
    return value, swap(value, "col", 1)


ROWS_PER_STEP = 2048
FIRST_ROWS_PER_STEP = 3072
BASIS_ROWS_PER_STEP = 1536


def shards(panel):
    total_rows = panel.shape[0] * lax.axis_size("row") * lax.axis_size("col")
    scale = float(total_rows) ** 0.5
    keep, send = gram_call(panel, ROWS_PER_STEP)
    w, upper = chol_one_call(*reduce_gram(keep, send))
    first, keep, send = first_call(panel, w, FIRST_ROWS_PER_STEP)
    small, c, factor = chol_two_call(*reduce_gram(keep, send), upper, scale)
    return basis_call(small, first, c, BASIS_ROWS_PER_STEP, scale), factor


def solution(mesh):
    return jax.shard_map(
        shards,
        mesh=mesh,
        in_specs=(P(("row", "col"), None),),
        out_specs=(P(("row", "col"), None), P()),
        check_vma=False,
    )
```

```python
import functools
import jax
import jax.numpy as jnp
from jax import lax
from jax.experimental import pallas as pl
from jax.experimental.pallas import tpu as pltpu
from jax.sharding import PartitionSpec as P

K = 256
H = 128
HALF = 136
F32 = jnp.float32
BF16 = jnp.bfloat16
VMEM_WHOLE = pl.BlockSpec(memory_space=pltpu.VMEM)


def params(mib):
    return pltpu.CompilerParams(vmem_limit_bytes=mib << 20)


def split2(x):
    hi = x.astype(BF16)
    return hi, (x - hi.astype(F32)).astype(BF16)


def split3(x):
    hi = x.astype(BF16)
    rest = x - hi.astype(F32)
    mid = rest.astype(BF16)
    return hi, mid, (rest - mid.astype(F32)).astype(BF16)


def dot_tn(a, b):
    return lax.dot_general(a, b, (((0,), (0,)), ((), ())), preferred_element_type=F32)


def dot_nn(a, b):
    return lax.dot_general(a, b, (((1,), (0,)), ((), ())), preferred_element_type=F32)


def dot_nt(a, b):
    return lax.dot_general(a, b, (((1,), (1,)), ((), ())), preferred_element_type=F32)


def iotas(shape):
    return lax.broadcasted_iota(jnp.int32, shape, 0), lax.broadcasted_iota(jnp.int32, shape, 1)


def core_index():
    return lax.rem(lax.axis_index("col"), 2)


def pack(gram, keep_ref, send_ref):
    i, j = iotas((H, H))
    low = gram[H:, H:]
    top = jnp.where(i >= j, gram[:H, :H], low)
    diag = jnp.sum(jnp.where(i == j, low, 0.0), axis=0, keepdims=True)
    tail = jnp.broadcast_to(diag, (8, H))
    core = core_index()

    def put(first_ref, second_ref):
        first_ref[0:H, :] = top
        first_ref[H:HALF, :] = tail
        second_ref[0:H, :] = gram[H:, :H]
        second_ref[H:HALF, :] = jnp.zeros((8, H), F32)

    @pl.when(core == 0)
    def _():
        put(keep_ref, send_ref)

    @pl.when(core == 1)
    def _():
        put(send_ref, keep_ref)


def unpack(mine_ref, other_ref, out_ref):
    core = core_index()
    i, j = iotas((H, H))

    def get(first_ref, second_ref):
        top = first_ref[0:H, :]
        topt = top.T
        diag = first_ref[H:H + 1, :]
        side = second_ref[0:H, :]
        out_ref[0:H, 0:H] = jnp.where(i >= j, top, topt)
        corner = jnp.where(i < j, top, topt)
        out_ref[H:, H:] = jnp.where(i == j, jnp.broadcast_to(diag, (H, H)), corner)
        out_ref[H:, 0:H] = side
        out_ref[0:H, H:] = side.T

    @pl.when(core == 0)
    def _():
        get(mine_ref, other_ref)

    @pl.when(core == 1)
    def _():
        get(other_ref, mine_ref)


def gram_kernel(rows, x_hbm, keep_ref, send_ref, x_ref, acc, sems):
    steps = x_hbm.shape[0] // rows

    def part(step):
        return pl.ds(pl.multiple_of(step * rows, rows), rows)

    def copy(step):
        return pltpu.make_async_copy(x_hbm.at[part(step)], x_ref.at[part(step)], sems.at[step])

    for step in range(steps):
        copy(step).start()
    acc[...] = jnp.zeros_like(acc)

    def body(step, carry):
        copy(step).wait()
        h, m = split2(x_ref[part(step), :])
        acc[:, : 2 * K] += dot_tn(h, jnp.concatenate([h, m], axis=1))
        acc[:, 2 * K :] += dot_tn(m, m)
        return carry

    lax.fori_loop(0, steps, body, 0)
    cross = acc[:, K : 2 * K]
    pack(acc[:, :K] + (cross + cross.T) + acc[:, 2 * K :], keep_ref, send_ref)


def gram_call(x, rows):
    half = jax.ShapeDtypeStruct((HALF, H), F32)
    return pl.pallas_call(
        functools.partial(gram_kernel, rows),
        out_shape=(half, half),
        in_specs=[pl.BlockSpec(memory_space=pltpu.HBM)],
        out_specs=[VMEM_WHOLE] * 2,
        scratch_shapes=[
            pltpu.VMEM(x.shape, F32),
            pltpu.VMEM((K, 3 * K), F32),
            pltpu.SemaphoreType.DMA((x.shape[0] // rows,)),
        ],
        compiler_params=params(52),
        name="gram_one",
    )(x)


def first_kernel(rows, x_hbm, w_ref, first_ref, keep_ref, send_ref, x_ref, acc, sems):
    steps = x_hbm.shape[0] // rows

    def copy(step):
        part = pl.ds(pl.multiple_of(step * rows, rows), rows)
        return pltpu.make_async_copy(x_hbm.at[part], x_ref.at[part], sems.at[step])

    for step in range(steps):
        copy(step).start()
    acc[...] = jnp.zeros_like(acc)

    def body(step, carry):
        copy(step).wait()
        total = None
        for n in range(2):
            part = pl.ds(pl.multiple_of(step * rows + n * (rows // 2), rows // 2), rows // 2)
            h, m, l = split3(x_ref[part, :])
            upper = jnp.concatenate([h[:, :H], m[:, :H], h[:, :H], m[:, :H], l], axis=1)
            lower = jnp.concatenate([h[:, H:], m[:, H:]], axis=1)
            first = dot_nn(upper, w_ref[: 3 * K, :])
            more = dot_nn(lower, w_ref[3 * K :, :])
            first = jnp.concatenate([first[:, :H], first[:, H:] + (more[:, :H] + more[:, H:])], axis=1)
            first_ref[part, :] = first
            fh, fm = split2(first)
            gram = dot_tn(fh, jnp.concatenate([fh, fm], axis=1))
            total = gram if total is None else total + gram
        acc[...] += total
        return carry

    lax.fori_loop(0, steps, body, 0)
    cross = acc[:, K:]
    pack(acc[:, :K] + (cross + cross.T), keep_ref, send_ref)


def first_call(x, w, rows):
    half = jax.ShapeDtypeStruct((HALF, H), F32)
    return pl.pallas_call(
        functools.partial(first_kernel, rows),
        out_shape=(jax.ShapeDtypeStruct(x.shape, F32), half, half),
        in_specs=[pl.BlockSpec(memory_space=pltpu.HBM), VMEM_WHOLE],
        out_specs=[VMEM_WHOLE] * 3,
        scratch_shapes=[
            pltpu.VMEM(x.shape, F32),
            pltpu.VMEM((K, 2 * K), F32),
            pltpu.SemaphoreType.DMA((x.shape[0] // rows,)),
        ],
        compiler_params=params(36),
        name="first_and_gram_two",
    )(x, w)


def basis_kernel(rows, scale, small_ref, f_ref, c_ref, out_hbm, out_ref, sems):
    steps = f_ref.shape[0] // rows

    def part(step):
        return pl.ds(pl.multiple_of(step * rows, rows), rows)

    def copy(step):
        return pltpu.make_async_copy(out_ref.at[part(step)], out_hbm.at[part(step)], sems.at[step])

    def run(correction):
        def body(step, carry):
            first = f_ref[part(step), :]
            out_ref[part(step), :] = (first + correction(first)) * scale
            copy(step).start()
            return carry

        lax.fori_loop(0, steps, body, 0)

    def one_product(first):
        return dot_nn(first.astype(BF16), c_ref[:K, :])

    def three_products(first):
        h, m = split2(first)
        return dot_nn(jnp.concatenate([h, m, h], axis=1), c_ref[...])

    @pl.when(small_ref[0] == 1)
    def _():
        run(one_product)

    @pl.when(small_ref[0] == 0)
    def _():
        run(three_products)

    for step in range(steps):
        copy(step).wait()


def basis_call(small, first, c, rows, scale):
    return pl.pallas_call(
        functools.partial(basis_kernel, rows, scale),
        out_shape=jax.ShapeDtypeStruct(first.shape, F32),
        in_specs=[pl.BlockSpec(memory_space=pltpu.SMEM)] + [VMEM_WHOLE] * 2,
        out_specs=pl.BlockSpec(memory_space=pltpu.HBM),
        scratch_shapes=[pltpu.VMEM(first.shape, F32), pltpu.SemaphoreType.DMA((first.shape[0] // rows,))],
        compiler_params=params(34),
        name="basis",
    )(small, first, c)


B = 32
S = 8


def eliminate(rows_a, lane0):
    rows_a = list(rows_a)
    width = rows_a[0].shape[1]
    sub = lax.broadcasted_iota(jnp.int32, (S, H), 0)

    def wide(v):
        return jnp.concatenate([v] * (width // H), axis=1)

    def columns(rows, s):
        return [jnp.broadcast_to(rows[:, lane0 + S * s + k : lane0 + S * s + k + 1], (S, H)) for k in range(S)]

    for s in range(B // S):
        x = rows_a[s]
        cols = columns(x, s)
        pivots, factors, us = [], [], []
        scales = None
        for j in range(S):
            r = jnp.broadcast_to(lax.rsqrt(cols[j][j : j + 1, :]), (S, H))
            lj = cols[j] * r
            fac = [None] * S
            for k in range(j + 1, S):
                fac[k] = jnp.broadcast_to(lj[k : k + 1, :], (S, H))
                cols[k] = cols[k] - lj * fac[k]
            u = jnp.broadcast_to(x[j : j + 1, :], (S, width)) * wide(r)
            if j < S - 1:
                x = x - wide(jnp.where(sub > j, lj, 0.0)) * u
            scales = r if scales is None else jnp.where(sub == j, r, scales)
            pivots.append(r)
            factors.append(fac)
            us.append(u)
        rows_a[s] = x * wide(scales)
        for q in range(s + 1, B // S):
            y = rows_a[q]
            c = columns(y, s)
            for j in range(S):
                lj = c[j] * pivots[j]
                for k in range(j + 1, S):
                    c[k] = c[k] - lj * factors[j][k]
                y = y - wide(lj) * us[j]
            rows_a[q] = y
    return jnp.concatenate(rows_a, axis=0)


def factorize(t_ref):
    for side in range(2):
        lanes = slice(side * H, side * H + 3 * H)
        width = K - side * H
        for lane0 in range(0, H, B):
            r0 = side * H + lane0
            r = t_ref[r0 : r0 + B, lanes]
            u = eliminate([r[S * s : S * s + S] for s in range(B // S)], lane0)
            t_ref[r0 : r0 + B, lanes] = u
            if r0 + B == K:
                break
            below = slice((r0 + B) // H * H, K)
            left = u[:, below.start - side * H : width]
            lane = lax.broadcasted_iota(jnp.int32, left.shape, 1) + below.start
            lh, lm, ll = split3(jnp.where(lane >= r0 + B, left, 0.0))
            uh, um, ul = split3(u)
            t_ref[below, lanes] -= dot_tn(
                jnp.concatenate([lh, lh, lm, lm, lh, ll], axis=0),
                jnp.concatenate([uh, um, uh, um, ul, uh], axis=0),
            )


def chol_one_kernel(mine_ref, other_ref, w_ref, upper_ref, t_ref):
    unpack(mine_ref, other_ref, t_ref.at[:, 0:K])
    i, j = iotas((K, K))
    t_ref[:, K:] = jnp.where(i == j, 1.0, 0.0)
    factorize(t_ref)
    upper_ref[...] = jnp.where(i <= j, t_ref[:, :K], 0.0)
    h, m = split2(jnp.where(i >= j, t_ref[:, K:], 0.0).T)
    for n in range(2):
        w_ref[n * H : (n + 1) * H, :] = h[:H]
        w_ref[(2 + n) * H : (3 + n) * H, :] = m[:H]
        w_ref[(6 + n) * H : (7 + n) * H, :] = jnp.concatenate([h[H:, H:], m[H:, H:]], axis=1)
    w_ref[2 * K : 3 * K, :] = h


def chol_one_call(mine, other):
    return pl.pallas_call(
        chol_one_kernel,
        out_shape=(jax.ShapeDtypeStruct((4 * K, K), BF16), jax.ShapeDtypeStruct((K, K), F32)),
        in_specs=[VMEM_WHOLE] * 2,
        out_specs=[VMEM_WHOLE] * 2,
        scratch_shapes=[pltpu.VMEM((K, 2 * K), F32)],
        compiler_params=params(16),
        name="factor_one",
    )(mine, other)


TOL = 1e-7
SMALL = 4e-3


def largest(x):
    return jnp.max(jnp.abs(x))


def chol_two_kernel(scale, mine_ref, other_ref, upper_ref, small_ref, c_ref, factor_ref, g_ref, x_ref, z_ref, t_ref):
    unpack(mine_ref, other_ref, g_ref)
    i, j = iotas((K, K))
    eye = jnp.where(i == j, 1.0, 0.0)
    half_low = jnp.where(i > j, 1.0, jnp.where(i == j, 0.5, 0.0))

    x_ref[...] = (g_ref[...] - eye) * half_low

    def x_more(state):
        step, ahead = state
        return jnp.logical_and(step < 10, jnp.logical_not(ahead <= TOL))

    def x_next(state):
        old = x_ref[...]
        h, m = split2(old)
        square = dot_nt(jnp.concatenate([h, h, m], axis=1), jnp.concatenate([h, m, h], axis=1))
        new = (g_ref[...] - eye - square) * half_low
        x_ref[...] = new
        rate = 2.0 * jnp.max(jnp.sum(jnp.abs(new), axis=1))
        return state[0] + 1, jnp.where(rate <= 0.5, largest(new - old) * rate, 1.0)

    _, ahead = lax.while_loop(x_more, x_next, (jnp.int32(0), jnp.float32(1.0)))
    x = x_ref[...]
    z_ref[...] = -x

    def residual():
        z = z_ref[...]
        xh, xm = split2(x_ref[...])
        zh, zm = split2(z)
        prod = dot_nn(jnp.concatenate([xh, xh, xm], axis=1), jnp.concatenate([zh, zm, zh], axis=0))
        return -(x_ref[...] + z + prod)

    def z_more(state):
        step, size = state
        return jnp.logical_and(step < 6, jnp.logical_not(size <= TOL))

    def z_next(state):
        r = residual()
        z = z_ref[...]
        rh, rm = split2(r)
        zh, zm = split2(z)
        z_ref[...] = z + r + dot_nn(jnp.concatenate([zh, zh, zm], axis=1), jnp.concatenate([rh, rm, rh], axis=0))
        return state[0] + 1, largest(r) * largest(r) * 256.0

    _, size = lax.while_loop(z_more, z_next, (jnp.int32(0), jnp.float32(1.0)))
    lowest = jnp.min(jnp.where(i == j, x, 0.0))
    good = jnp.logical_and(jnp.logical_and(ahead <= TOL, size <= TOL), lowest > -0.5)

    @pl.when(jnp.logical_not(good))
    def _():
        t_ref[:, :K] = g_ref[...]
        t_ref[:, K:] = eye
        factorize(t_ref)
        x_ref[...] = jnp.where(i <= j, t_ref[:, :K], 0.0).T - eye
        z_ref[...] = jnp.where(i >= j, t_ref[:, K:], 0.0) - eye

    z = z_ref[...]
    small_ref[0] = (jnp.sum(z * z) <= SMALL * SMALL * K).astype(jnp.int32)
    ch, cm = split2(z.T)
    c_ref[0:K, :] = ch
    c_ref[K:2 * K, :] = ch
    c_ref[2 * K:3 * K, :] = cm
    u1 = upper_ref[...]
    uh, um = split2(u1)
    xh, xm = split2(x_ref[...])
    prod = dot_tn(jnp.concatenate([xh, xh, xm], axis=0), jnp.concatenate([uh, um, uh], axis=0))
    factor_ref[...] = (u1 + prod) / scale


def chol_two_call(mine, other, upper, scale):
    return pl.pallas_call(
        functools.partial(chol_two_kernel, scale),
        out_shape=(
            jax.ShapeDtypeStruct((1,), jnp.int32),
            jax.ShapeDtypeStruct((3 * K, K), BF16),
            jax.ShapeDtypeStruct((K, K), F32),
        ),
        in_specs=[VMEM_WHOLE] * 3,
        out_specs=[pl.BlockSpec(memory_space=pltpu.SMEM)] + [VMEM_WHOLE] * 2,
        scratch_shapes=[pltpu.VMEM((K, K), F32)] * 3 + [pltpu.VMEM((K, 2 * K), F32)],
        compiler_params=params(16),
        name="factor_two",
    )(mine, other, upper)


def swap(value, axis, distance):
    return lax.ppermute(value, axis, [(i, i ^ distance) for i in range(lax.axis_size(axis))])


def sum_over(value, axis, step):
    a, b, c = [swap(value, axis, step * d) for d in (1, 2, 3)]
    return (value + a) + (b + c)


def reduce_gram(keep, send):
    value = keep + swap(send, "col", 1)
    value = sum_over(value, "col", 2)
    value = sum_over(value, "row", 1)
    value = sum_over(value, "row", 4)
    return value, swap(value, "col", 1)


ROWS_PER_STEP = 2048
FIRST_ROWS_PER_STEP = 3072
BASIS_ROWS_PER_STEP = 1536


def shards(panel):
    total_rows = panel.shape[0] * lax.axis_size("row") * lax.axis_size("col")
    scale = float(total_rows) ** 0.5
    keep, send = gram_call(panel, ROWS_PER_STEP)
    w, upper = chol_one_call(*reduce_gram(keep, send))
    first, keep, send = first_call(panel, w, FIRST_ROWS_PER_STEP)
    small, c, factor = chol_two_call(*reduce_gram(keep, send), upper, scale)
    return basis_call(small, first, c, BASIS_ROWS_PER_STEP, scale), factor


def solution(mesh):
    return jax.shard_map(
        shards,
        mesh=mesh,
        in_specs=(P(("row", "col"), None),),
        out_specs=(P(("row", "col"), None), P()),
        check_vma=False,
    )
```

```python
import functools
import jax
import jax.numpy as jnp
from jax import lax
from jax.experimental import pallas as pl
from jax.experimental.pallas import tpu as pltpu
from jax.sharding import PartitionSpec as P

K = 256
H = 128
HALF = 136
F32 = jnp.float32
BF16 = jnp.bfloat16
VMEM_WHOLE = pl.BlockSpec(memory_space=pltpu.VMEM)


def params(mib):
    return pltpu.CompilerParams(vmem_limit_bytes=mib << 20)


def split2(x):
    hi = x.astype(BF16)
    return hi, (x - hi.astype(F32)).astype(BF16)


def split3(x):
    hi = x.astype(BF16)
    rest = x - hi.astype(F32)
    mid = rest.astype(BF16)
    return hi, mid, (rest - mid.astype(F32)).astype(BF16)


def dot_tn(a, b):
    return lax.dot_general(a, b, (((0,), (0,)), ((), ())), preferred_element_type=F32)


def dot_nn(a, b):
    return lax.dot_general(a, b, (((1,), (0,)), ((), ())), preferred_element_type=F32)


def dot_nt(a, b):
    return lax.dot_general(a, b, (((1,), (1,)), ((), ())), preferred_element_type=F32)


def iotas(shape):
    return lax.broadcasted_iota(jnp.int32, shape, 0), lax.broadcasted_iota(jnp.int32, shape, 1)


def core_index():
    return lax.rem(lax.axis_index("col"), 2)


def pack(gram, keep_ref, send_ref):
    i, j = iotas((H, H))
    low = gram[H:, H:]
    top = jnp.where(i >= j, gram[:H, :H], low)
    diag = jnp.sum(jnp.where(i == j, low, 0.0), axis=0, keepdims=True)
    tail = jnp.broadcast_to(diag, (8, H))
    core = core_index()

    def put(first_ref, second_ref):
        first_ref[0:H, :] = top
        first_ref[H:HALF, :] = tail
        second_ref[0:H, :] = gram[H:, :H]
        second_ref[H:HALF, :] = jnp.zeros((8, H), F32)

    @pl.when(core == 0)
    def _():
        put(keep_ref, send_ref)

    @pl.when(core == 1)
    def _():
        put(send_ref, keep_ref)


def unpack(mine_ref, other_ref, out_ref):
    core = core_index()
    i, j = iotas((H, H))

    def get(first_ref, second_ref):
        top = first_ref[0:H, :]
        topt = top.T
        diag = first_ref[H:H + 1, :]
        side = second_ref[0:H, :]
        out_ref[0:H, 0:H] = jnp.where(i >= j, top, topt)
        corner = jnp.where(i < j, top, topt)
        out_ref[H:, H:] = jnp.where(i == j, jnp.broadcast_to(diag, (H, H)), corner)
        out_ref[H:, 0:H] = side
        out_ref[0:H, H:] = side.T

    @pl.when(core == 0)
    def _():
        get(mine_ref, other_ref)

    @pl.when(core == 1)
    def _():
        get(other_ref, mine_ref)


def gram_kernel(rows, x_hbm, keep_ref, send_ref, x_ref, acc, sems):
    steps = x_hbm.shape[0] // rows

    def part(step):
        return pl.ds(pl.multiple_of(step * rows, rows), rows)

    def copy(step):
        return pltpu.make_async_copy(x_hbm.at[part(step)], x_ref.at[part(step)], sems.at[step])

    for step in range(steps):
        copy(step).start()
    acc[...] = jnp.zeros_like(acc)

    def body(step, carry):
        copy(step).wait()
        h, m = split2(x_ref[part(step), :])
        acc[:, : 2 * K] += dot_tn(h, jnp.concatenate([h, m], axis=1))
        acc[:, 2 * K :] += dot_tn(m, m)
        return carry

    lax.fori_loop(0, steps, body, 0)
    cross = acc[:, K : 2 * K]
    pack(acc[:, :K] + (cross + cross.T) + acc[:, 2 * K :], keep_ref, send_ref)


def gram_call(x, rows):
    half = jax.ShapeDtypeStruct((HALF, H), F32)
    return pl.pallas_call(
        functools.partial(gram_kernel, rows),
        out_shape=(half, half),
        in_specs=[pl.BlockSpec(memory_space=pltpu.HBM)],
        out_specs=[VMEM_WHOLE] * 2,
        scratch_shapes=[
            pltpu.VMEM(x.shape, F32),
            pltpu.VMEM((K, 3 * K), F32),
            pltpu.SemaphoreType.DMA((x.shape[0] // rows,)),
        ],
        compiler_params=params(52),
        name="gram_one",
    )(x)


def first_kernel(rows, x_hbm, w_ref, first_ref, keep_ref, send_ref, x_ref, acc, sems):
    steps = x_hbm.shape[0] // rows

    def copy(step):
        part = pl.ds(pl.multiple_of(step * rows, rows), rows)
        return pltpu.make_async_copy(x_hbm.at[part], x_ref.at[part], sems.at[step])

    for step in range(steps):
        copy(step).start()
    acc[...] = jnp.zeros_like(acc)

    def body(step, carry):
        copy(step).wait()
        total = None
        for n in range(2):
            part = pl.ds(pl.multiple_of(step * rows + n * (rows // 2), rows // 2), rows // 2)
            h, m, l = split3(x_ref[part, :])
            upper = jnp.concatenate([h[:, :H], m[:, :H], h[:, :H], m[:, :H], l], axis=1)
            lower = jnp.concatenate([h[:, H:], m[:, H:]], axis=1)
            first = dot_nn(upper, w_ref[: 3 * K, :])
            more = dot_nn(lower, w_ref[3 * K :, :])
            first = jnp.concatenate([first[:, :H], first[:, H:] + (more[:, :H] + more[:, H:])], axis=1)
            first_ref[part, :] = first
            fh, fm = split2(first)
            gram = dot_tn(fh, jnp.concatenate([fh, fm], axis=1))
            total = gram if total is None else total + gram
        acc[...] += total
        return carry

    lax.fori_loop(0, steps, body, 0)
    cross = acc[:, K:]
    pack(acc[:, :K] + (cross + cross.T), keep_ref, send_ref)


def first_call(x, w, rows):
    half = jax.ShapeDtypeStruct((HALF, H), F32)
    return pl.pallas_call(
        functools.partial(first_kernel, rows),
        out_shape=(jax.ShapeDtypeStruct(x.shape, F32), half, half),
        in_specs=[pl.BlockSpec(memory_space=pltpu.HBM), VMEM_WHOLE],
        out_specs=[VMEM_WHOLE] * 3,
        scratch_shapes=[
            pltpu.VMEM(x.shape, F32),
            pltpu.VMEM((K, 2 * K), F32),
            pltpu.SemaphoreType.DMA((x.shape[0] // rows,)),
        ],
        compiler_params=params(36),
        name="first_and_gram_two",
    )(x, w)


def basis_kernel(rows, scale, small_ref, f_ref, c_ref, out_hbm, out_ref, sems):
    steps = f_ref.shape[0] // rows

    def part(step):
        return pl.ds(pl.multiple_of(step * rows, rows), rows)

    def copy(step):
        return pltpu.make_async_copy(out_ref.at[part(step)], out_hbm.at[part(step)], sems.at[step])

    def run(correction):
        def body(step, carry):
            first = f_ref[part(step), :]
            out_ref[part(step), :] = (first + correction(first)) * scale
            copy(step).start()
            return carry

        lax.fori_loop(0, steps, body, 0)

    def one_product(first):
        return dot_nn(first.astype(BF16), c_ref[:K, :])

    def three_products(first):
        h, m = split2(first)
        return dot_nn(jnp.concatenate([h, m, h], axis=1), c_ref[...])

    @pl.when(small_ref[0] == 1)
    def _():
        run(one_product)

    @pl.when(small_ref[0] == 0)
    def _():
        run(three_products)

    for step in range(steps):
        copy(step).wait()


def basis_call(small, first, c, rows, scale):
    return pl.pallas_call(
        functools.partial(basis_kernel, rows, scale),
        out_shape=jax.ShapeDtypeStruct(first.shape, F32),
        in_specs=[pl.BlockSpec(memory_space=pltpu.SMEM)] + [VMEM_WHOLE] * 2,
        out_specs=pl.BlockSpec(memory_space=pltpu.HBM),
        scratch_shapes=[pltpu.VMEM(first.shape, F32), pltpu.SemaphoreType.DMA((first.shape[0] // rows,))],
        compiler_params=params(34),
        name="basis",
    )(small, first, c)


B = 32
S = 8


def eliminate(rows_a, lane0):
    rows_a = list(rows_a)
    width = rows_a[0].shape[1]
    sub = lax.broadcasted_iota(jnp.int32, (S, H), 0)

    def wide(v):
        return jnp.concatenate([v] * (width // H), axis=1)

    def columns(rows, s):
        return [jnp.broadcast_to(rows[:, lane0 + S * s + k : lane0 + S * s + k + 1], (S, H)) for k in range(S)]

    for s in range(B // S):
        x = rows_a[s]
        cols = columns(x, s)
        pivots, factors, us = [], [], []
        scales = None
        for j in range(S):
            r = jnp.broadcast_to(lax.rsqrt(cols[j][j : j + 1, :]), (S, H))
            lj = cols[j] * r
            fac = [None] * S
            for k in range(j + 1, S):
                fac[k] = jnp.broadcast_to(lj[k : k + 1, :], (S, H))
                cols[k] = cols[k] - lj * fac[k]
            u = jnp.broadcast_to(x[j : j + 1, :], (S, width)) * wide(r)
            if j < S - 1:
                x = x - wide(jnp.where(sub > j, lj, 0.0)) * u
            scales = r if scales is None else jnp.where(sub == j, r, scales)
            pivots.append(r)
            factors.append(fac)
            us.append(u)
        rows_a[s] = x * wide(scales)
        for q in range(s + 1, B // S):
            y = rows_a[q]
            c = columns(y, s)
            for j in range(S):
                lj = c[j] * pivots[j]
                for k in range(j + 1, S):
                    c[k] = c[k] - lj * factors[j][k]
                y = y - wide(lj) * us[j]
            rows_a[q] = y
    return jnp.concatenate(rows_a, axis=0)


def factorize(t_ref):
    for side in range(2):
        lanes = slice(side * H, side * H + 3 * H)
        width = K - side * H
        for lane0 in range(0, H, B):
            r0 = side * H + lane0
            r = t_ref[r0 : r0 + B, lanes]
            u = eliminate([r[S * s : S * s + S] for s in range(B // S)], lane0)
            t_ref[r0 : r0 + B, lanes] = u
            if r0 + B == K:
                break
            below = slice((r0 + B) // H * H, K)
            left = u[:, below.start - side * H : width]
            lane = lax.broadcasted_iota(jnp.int32, left.shape, 1) + below.start
            lh, lm, ll = split3(jnp.where(lane >= r0 + B, left, 0.0))
            uh, um, ul = split3(u)
            t_ref[below, lanes] -= dot_tn(
                jnp.concatenate([lh, lh, lm, lm, lh, ll], axis=0),
                jnp.concatenate([uh, um, uh, um, ul, uh], axis=0),
            )


def chol_one_kernel(mine_ref, other_ref, w_ref, upper_ref, t_ref):
    unpack(mine_ref, other_ref, t_ref.at[:, 0:K])
    i, j = iotas((K, K))
    t_ref[:, K:] = jnp.where(i == j, 1.0, 0.0)
    factorize(t_ref)
    upper_ref[...] = jnp.where(i <= j, t_ref[:, :K], 0.0)
    h, m = split2(jnp.where(i >= j, t_ref[:, K:], 0.0).T)
    for n in range(2):
        w_ref[n * H : (n + 1) * H, :] = h[:H]
        w_ref[(2 + n) * H : (3 + n) * H, :] = m[:H]
        w_ref[(6 + n) * H : (7 + n) * H, :] = jnp.concatenate([h[H:, H:], m[H:, H:]], axis=1)
    w_ref[2 * K : 3 * K, :] = h


def chol_one_call(mine, other):
    return pl.pallas_call(
        chol_one_kernel,
        out_shape=(jax.ShapeDtypeStruct((4 * K, K), BF16), jax.ShapeDtypeStruct((K, K), F32)),
        in_specs=[VMEM_WHOLE] * 2,
        out_specs=[VMEM_WHOLE] * 2,
        scratch_shapes=[pltpu.VMEM((K, 2 * K), F32)],
        compiler_params=params(16),
        name="factor_one",
    )(mine, other)


TOL = 1e-7
SMALL = 4e-3


def largest(x):
    return jnp.max(jnp.abs(x))


def chol_two_kernel(scale, mine_ref, other_ref, upper_ref, small_ref, c_ref, factor_ref, g_ref, x_ref, z_ref, t_ref):
    unpack(mine_ref, other_ref, g_ref)
    i, j = iotas((K, K))
    eye = jnp.where(i == j, 1.0, 0.0)
    half_low = jnp.where(i > j, 1.0, jnp.where(i == j, 0.5, 0.0))

    x_ref[...] = (g_ref[...] - eye) * half_low

    def x_more(state):
        step, ahead = state
        return jnp.logical_and(step < 10, jnp.logical_not(ahead <= TOL))

    def x_next(state):
        old = x_ref[...]
        h, m = split2(old)
        square = dot_nt(jnp.concatenate([h, h, m], axis=1), jnp.concatenate([h, m, h], axis=1))
        new = (g_ref[...] - eye - square) * half_low
        x_ref[...] = new
        rate = 2.0 * jnp.max(jnp.sum(jnp.abs(new), axis=1))
        return state[0] + 1, jnp.where(rate <= 0.5, largest(new - old) * rate, 1.0)

    _, ahead = lax.while_loop(x_more, x_next, (jnp.int32(0), jnp.float32(1.0)))
    x = x_ref[...]
    z_ref[...] = -x

    def residual():
        z = z_ref[...]
        xh, xm = split2(x_ref[...])
        zh, zm = split2(z)
        prod = dot_nn(jnp.concatenate([xh, xh, xm], axis=1), jnp.concatenate([zh, zm, zh], axis=0))
        return -(x_ref[...] + z + prod)

    def z_more(state):
        step, size = state
        return jnp.logical_and(step < 6, jnp.logical_not(size <= TOL))

    def z_next(state):
        r = residual()
        z = z_ref[...]
        rh, rm = split2(r)
        zh, zm = split2(z)
        z_ref[...] = z + r + dot_nn(jnp.concatenate([zh, zh, zm], axis=1), jnp.concatenate([rh, rm, rh], axis=0))
        return state[0] + 1, largest(r) * largest(r) * 256.0

    _, size = lax.while_loop(z_more, z_next, (jnp.int32(0), jnp.float32(1.0)))
    lowest = jnp.min(jnp.where(i == j, x, 0.0))
    good = jnp.logical_and(jnp.logical_and(ahead <= TOL, size <= TOL), lowest > -0.5)

    @pl.when(jnp.logical_not(good))
    def _():
        t_ref[:, :K] = g_ref[...]
        t_ref[:, K:] = eye
        factorize(t_ref)
        x_ref[...] = jnp.where(i <= j, t_ref[:, :K], 0.0).T - eye
        z_ref[...] = jnp.where(i >= j, t_ref[:, K:], 0.0) - eye

    z = z_ref[...]
    small_ref[0] = (jnp.sum(z * z) <= SMALL * SMALL * K).astype(jnp.int32)
    ch, cm = split2(z.T)
    c_ref[0:K, :] = ch
    c_ref[K:2 * K, :] = ch
    c_ref[2 * K:3 * K, :] = cm
    u1 = upper_ref[...]
    uh, um = split2(u1)
    xh, xm = split2(x_ref[...])
    prod = dot_tn(jnp.concatenate([xh, xh, xm], axis=0), jnp.concatenate([uh, um, uh], axis=0))
    factor_ref[...] = (u1 + prod) / scale


def chol_two_call(mine, other, upper, scale):
    return pl.pallas_call(
        functools.partial(chol_two_kernel, scale),
        out_shape=(
            jax.ShapeDtypeStruct((1,), jnp.int32),
            jax.ShapeDtypeStruct((3 * K, K), BF16),
            jax.ShapeDtypeStruct((K, K), F32),
        ),
        in_specs=[VMEM_WHOLE] * 3,
        out_specs=[pl.BlockSpec(memory_space=pltpu.SMEM)] + [VMEM_WHOLE] * 2,
        scratch_shapes=[pltpu.VMEM((K, K), F32)] * 3 + [pltpu.VMEM((K, 2 * K), F32)],
        compiler_params=params(16),
        name="factor_two",
    )(mine, other, upper)


def swap(value, axis, distance):
    return lax.ppermute(value, axis, [(i, i ^ distance) for i in range(lax.axis_size(axis))])


def sum_over(value, axis, step):
    a, b, c = [swap(value, axis, step * d) for d in (1, 2, 3)]
    return (value + a) + (b + c)


def reduce_gram(keep, send):
    value = keep + swap(send, "col", 1)
    value = sum_over(value, "col", 2)
    value = sum_over(value, "row", 1)
    value = sum_over(value, "row", 4)
    return value, swap(value, "col", 1)


ROWS_PER_STEP = 1536
FIRST_ROWS_PER_STEP = 3072
BASIS_ROWS_PER_STEP = 1536


def shards(panel):
    total_rows = panel.shape[0] * lax.axis_size("row") * lax.axis_size("col")
    scale = float(total_rows) ** 0.5
    keep, send = gram_call(panel, ROWS_PER_STEP)
    w, upper = chol_one_call(*reduce_gram(keep, send))
    first, keep, send = first_call(panel, w, FIRST_ROWS_PER_STEP)
    small, c, factor = chol_two_call(*reduce_gram(keep, send), upper, scale)
    return basis_call(small, first, c, BASIS_ROWS_PER_STEP, scale), factor


def solution(mesh):
    return jax.shard_map(
        shards,
        mesh=mesh,
        in_specs=(P(("row", "col"), None),),
        out_specs=(P(("row", "col"), None), P()),
        check_vma=False,
    )
```
